32 devices in a mesh: sub: 8 (over y, x, core), col: 4 (over z).
Axes of the slice: x: 2, y: 2, z: 4, core: 2. Of those that a mesh axis runs over, the one named last changes fastest.
Arguments:
- state_init: float32 [128, 8192], P('col', 'sub'), may hold values from -3 to 3
- load_cols: float32 [128, 8192], P('col', 'sub'), may hold values from -6 to 6
- stiff_diag: bfloat16 [1024, 8192], P(None, 'sub'), may hold values from -0.1875 to 0.1875
- stiff_rim: bfloat16 [1024, 8192], P(None, 'sub'), may hold values from -0.1875 to 0.1875
- inverse: bfloat16 [2048, 8192], P(None, 'sub'), may hold values from -0.125 to 0.125
- ov_rows: int32 [8, 1024], P('sub'), may hold values from 0 to 1023, as said below
- ov_count: int32 [8], P('sub'), may hold values from 512 to 1024, as said below
- coarse_basis: bfloat16 [8192, 192], P('sub'), may hold values from -0.1875 to 0.1875
- coarse_map: bfloat16 [1536, 1536], P('sub', 'col'), may hold values from -0.21875 to 0.21875
Outputs:
- solution: float32 [128, 8192], P('col', 'sub')
- residual: float32 [128, 8192], P('col', 'sub')
The draws below stay inside these ranges and needn't reach their ends.
Inputs may be any that keep to these rules, and one draw needn't show every extreme that they name: `ov_rows`: each row holds 1024 different rim positions. `ov_count`: some subdomain uses all 1024 margin slots in every draw.
All inputs are finite; a program needn't handle non-finite values.
Results may differ from the reference program's by a relative error of at most 0.0075.
Values may be sent and summed in bfloat16 or wider, within the bound.
A program may use at most 64 MiB of HBM per device.

```python
import jax
import jax.numpy as jnp
from jax import lax

R = 1024
H = 512
OV = 1024
SMAX = 2048
NC = 192
ITERS = 2
N_ROWS = 8192
K = 128
NCOARSE = 1536
N_SUB = 8
N_COL = 4


def draw_ov_rows(key, part):
    keys = jax.random.split(jax.random.fold_in(key, 11), N_SUB)
    return jax.vmap(lambda single: jax.random.permutation(single, 2 * H)[:OV])(keys).astype(jnp.int32)


def draw_ov_count(key, part):
    first_key, second_key = jax.random.split(jax.random.fold_in(key, 23))
    counts = jax.random.randint(first_key, (N_SUB,), OV // 2, OV + 1)
    fullest = jax.random.randint(second_key, (), 0, N_SUB)
    return jnp.where(jnp.arange(N_SUB) == fullest, OV, counts).astype(jnp.int32)


def strengthened(array, stream_key, source, target, blocks, factor):
    owner, partner = [(jnp.arange(array.shape[axis_at]) // (array.shape[axis_at] // blocks)).reshape([-1 if axis == axis_at else 1 for axis in range(array.ndim)]) for axis_at in (source, target)]
    chosen = jax.random.permutation(stream_key, blocks)[partner]
    strong = (owner == chosen) | (owner == (partner + blocks // 2) % blocks)
    return jnp.where(strong, factor * array, array)


def shard_levels(rng, dims, shards, smallest, largest):
    factor_of = 1.0
    for dim, blocks in shards:
        steps = jax.random.uniform(jax.random.fold_in(jax.random.fold_in(rng, 6), dim), (blocks,), jnp.float32, smallest / len(shards), largest / len(shards))
        factor_of = factor_of * jnp.repeat(jnp.exp(steps), dims[dim] // blocks).reshape((-1,) + (1,) * (len(dims) - 1 - dim))
    return factor_of


def centred(own_key, extent, width, limit, cuts=(), kind=jnp.bfloat16):
    loudness = shard_levels(own_key, extent, cuts, -0.22, 0.18) if cuts else 1.0
    values = jax.random.normal(own_key, extent, jnp.float32) * width * loudness
    return jnp.minimum(jnp.maximum(values, -limit), limit).astype(kind)


def gaussian_with(key, extent, spread, limit, cuts, heavy, kind=jnp.bfloat16):
    values = spread * jax.random.normal(key, extent, jnp.float32)
    if cuts:
        values = values * shard_levels(key, extent, cuts, -0.22, 0.18)
    return jnp.clip(strengthened(values, jax.random.fold_in(key, 3), *heavy), -limit, limit).astype(kind)


def setup_inputs(seed: int = 0) -> dict:
    key_list = jax.random.split(jax.random.key(seed), 10)
    return {
        "state_init": centred(key_list[0], (K, N_ROWS), 0.5, 3.0, ((0, 4), (1, 8)), jnp.float32),
        "load_cols": centred(key_list[1], (K, N_ROWS), 1.0, 6.0, ((0, 4), (1, 8)), jnp.float32),
        "stiff_diag": centred(key_list[2], (R, N_ROWS), R ** -0.5, 0.1875, ((1, 8),)),
        "stiff_rim": centred(key_list[3], (2 * H, N_ROWS), (2 * H) ** -0.5, 0.1875, ((1, 8),)),
        "inverse": centred(key_list[4], (SMAX, N_ROWS), SMAX ** -0.5, 0.125, ((1, 8),)),
        "ov_rows": draw_ov_rows(jax.random.fold_in(key_list[9], 71), 0),
        "ov_count": draw_ov_count(jax.random.fold_in(key_list[9], 71), 0),
        "coarse_basis": centred(key_list[7], (N_ROWS, NC), R ** -0.5, 0.1875, ((0, 8),)),
        "coarse_map": gaussian_with(key_list[8], (NCOARSE, NCOARSE), NCOARSE ** -0.5, 0.21875, ((0, 8), (1, 4)), (0, 1, 8, 2.0)),
    }


cubic_coef = 0.1


def to_bf16(values):
    return lax.optimization_barrier(values.astype(jnp.bfloat16)).astype(jnp.float32)


def neighbour_rims(blocks):
    edge = jnp.zeros_like(blocks[:, :1, :H])
    before = jnp.concatenate([edge, blocks[:, :-1, R - H:]], axis=1)
    after = jnp.concatenate([blocks[:, 1:, :H], edge], axis=1)
    return jnp.concatenate([before, after], axis=2)


def residual_of(current, load_cols, diag_blocks, rim_blocks):
    columns = current.shape[0]
    rounded = to_bf16(current).reshape(columns, N_SUB, R)
    border = neighbour_rims(rounded)
    applied = jnp.einsum('ksi,isj->ksj', rounded, diag_blocks) + jnp.einsum('ksi,isj->ksj', border, rim_blocks)
    return load_cols - applied.reshape(columns, N_SUB * R) - cubic_coef * current * current * current


def reference(state_init, load_cols, stiff_diag, stiff_rim, inverse, ov_rows, ov_count, coarse_basis, coarse_map):
    diag_blocks = stiff_diag.astype(jnp.float32).reshape(R, N_SUB, R)
    rim_blocks = stiff_rim.astype(jnp.float32).reshape(2 * H, N_SUB, R)
    solve_blocks = inverse.astype(jnp.float32).reshape(SMAX, N_SUB, R)
    basis_blocks = coarse_basis.astype(jnp.float32).reshape(N_SUB, R, NC)
    live = jnp.arange(OV, dtype=jnp.int32)[None, :] < ov_count[:, None]
    current = state_init
    columns = current.shape[0]
    for iteration in range(ITERS):
        residual_now = residual_of(current, load_cols, diag_blocks, rim_blocks)
        rounded = to_bf16(residual_now).reshape(columns, N_SUB, R)
        border = neighbour_rims(rounded)
        positions = jnp.broadcast_to(ov_rows[None], (columns, N_SUB, OV)).astype(jnp.int32)
        picked = jnp.take_along_axis(border, positions, axis=2)
        picked = jnp.where(live[None], picked, jnp.zeros_like(picked))
        local_rhs = jnp.concatenate([rounded, picked], axis=2)
        fine_part = jnp.einsum('ksi,isj->ksj', local_rhs, solve_blocks)
        coefficients = jnp.einsum('ksi,sic->ksc', rounded, basis_blocks)
        coefficients = coefficients.reshape(columns, N_SUB * NC).astype(jnp.bfloat16)
        coarse = jnp.dot(coefficients, coarse_map, preferred_element_type=jnp.float32)
        coarse = to_bf16(coarse).reshape(columns, N_COL, N_SUB, NC // N_COL)
        coarse = jnp.transpose(coarse, (0, 2, 1, 3)).reshape(columns, N_SUB, NC)
        coarse_lift = jnp.einsum('ksc,sic->ksi', coarse, basis_blocks)
        current = current + (fine_part + coarse_lift).reshape(columns, N_SUB * R)
    final_residual = residual_of(current, load_cols, diag_blocks, rim_blocks)
    return current, final_residual
```

```python
import functools

import jax
import jax.numpy as jnp
from jax import lax
from jax.experimental import pallas as pl
from jax.experimental.pallas import tpu as pltpu
from jax.sharding import PartitionSpec as P

ITERS = 2
PIECES = 4

cubic_coef = 0.1
MESH = pl.DeviceIdType.MESH
F32 = jnp.float32
BF16 = jnp.bfloat16


TAIL = 64
LANES = 128


def dot(a, b):
    return jnp.dot(a, b, preferred_element_type=F32)


def dot_nt(a, b):
    return lax.dot_general(a, b, (((1,), (1,)), ((), ())), preferred_element_type=F32)


def diagonal(size):
    place = [lax.broadcasted_iota(jnp.int32, (size, size), axis) for axis in (0, 1)]
    return (place[0] == place[1]).astype(F32).astype(BF16)


def lanes_of(value):
    return lax.broadcasted_iota(jnp.int32, value.shape, 1)


def fold(wide, full):
    half = wide.shape[0] // 2
    tail = wide[:, full * LANES :]
    low = lanes_of(tail[:half]) < TAIL
    tail = jnp.where(low, tail[:half], tail[half:])
    return jnp.concatenate([wide[:, f * LANES : (f + 1) * LANES] for f in range(full)] + [tail], axis=0)


def unfold(packed, rows, full):
    tail = packed[rows * full :]
    tail = jnp.concatenate([tail, tail], axis=0)
    upper = lax.broadcasted_iota(jnp.int32, tail.shape, 0) < rows // 2
    tail = jnp.where(upper == (lanes_of(tail) < TAIL), tail, jnp.zeros_like(tail))
    return jnp.concatenate([packed[f * rows : (f + 1) * rows] for f in range(full)] + [tail], axis=1)


def kernel(
    n, m,
    state_hbm, load_hbm, diag_hbm, rim_hbm, inv_hbm, ov_hbm, count_hbm, basis_hbm, map_hbm,
    before_ref, change_ref, applied_ref,
    cur, load, diag, rim, inv, ov, count, basis, near, lifted, own, maps, invp,
    sent, halo, part_out, part_in,
    local_sem, halo_send, halo_recv, near_send, near_recv, map_send, map_recv, relay_send, part_send, part_recv, entered,
):
    me_s = lax.axis_index("sub")
    me_c = lax.axis_index("col")
    rows, width = cur.shape
    h = halo.shape[3]
    nc = near.shape[1]
    per = nc // m
    full = nc // LANES
    slots = ov.shape[1]
    half = inv.shape[0] - slots
    relayed = m >= 4
    reach = m - 1 - relayed

    barrier = pltpu.get_barrier_semaphore()
    for k in range(1, n):
        pl.semaphore_signal(barrier, inc=1, device_id={"sub": lax.rem(me_s + k, n)}, device_id_type=MESH)
    for gap in range(1, reach + 1):
        @pl.when(me_c + gap < m)
        def _():
            pl.semaphore_signal(barrier, inc=1, device_id={"col": me_c + gap}, device_id_type=MESH)

    def fetch(index, source, target):
        copy = pltpu.make_async_copy(source, target, local_sem.at[index])
        copy.start()
        return copy

    get_state = fetch(0, state_hbm, cur)
    get_map = fetch(1, map_hbm, own)
    get_diag = fetch(2, diag_hbm, diag)
    get_basis = fetch(3, basis_hbm, basis.at[pl.ds(0, nc)])
    get_again = fetch(4, basis_hbm.at[pl.ds(nc - TAIL, TAIL)], basis.at[pl.ds(nc, TAIL)])
    get_rim = fetch(5, rim_hbm, rim)
    get_load = fetch(6, load_hbm, load)
    get_ov = fetch(7, ov_hbm, ov)
    get_count = fetch(8, count_hbm, count)
    get_inv = fetch(9, inv_hbm, inv)

    for side, edge in ((0, 0), (1, n - 1)):
        @pl.when(me_s == edge)
        def _():
            near[side] = jnp.zeros(near.shape[1:], BF16)
            for e in range(2 * ITERS + 1):
                halo[e, side] = jnp.zeros((rows, h), BF16)
    for it in range(ITERS):
        for edge in (0, n + 1):
            part_out[it, edge] = jnp.zeros(part_out.shape[2:], BF16)

    def trade(source, target, send, recv, side):
        step = 1 if side == 0 else n - 1
        return pltpu.make_async_remote_copy(
            src_ref=source, dst_ref=target, send_sem=send, recv_sem=recv,
            device_id={"sub": lax.rem(me_s + step, n)}, device_id_type=MESH)

    def halo_copy(e, side):
        at = width - h if side == 0 else 0
        return trade(
            sent.at[e, :, pl.ds(at, h)], halo.at[e, side], halo_send.at[e, side], halo_recv.at[e, side], side)

    def near_copy(e, side):
        at = width - h if side == 0 else 0
        return trade(basis.at[pl.ds(0, nc), pl.ds(at, h)], near.at[side], near_send.at[side], near_recv.at[side], side)

    def outward(copy, e, act):
        @pl.when(me_s < n - 1)
        def _():
            act(copy(e, 0))

        @pl.when(me_s > 0)
        def _():
            act(copy(e, 1))

    def inward(copy, e):
        @pl.when(me_s > 0)
        def _():
            copy(e, 0).wait_recv()

        @pl.when(me_s < n - 1)
        def _():
            copy(e, 1).wait_recv()

    def begin(copy):
        copy.start()

    def finish(copy):
        copy.wait_send()

    pieces = PIECES if relayed and maps.shape[1] % (16 * PIECES) == 0 else 1
    tall = maps.shape[1] // pieces

    def map_copy(peer, slot, piece, send):
        part = maps.at[slot, pl.ds(piece * tall, tall), :]
        return pltpu.make_async_remote_copy(
            src_ref=part, dst_ref=part, send_sem=send, recv_sem=map_recv.at[slot, piece],
            device_id={"col": peer}, device_id_type=MESH)

    def own_copy(peer, piece):
        return map_copy(peer, me_c, piece, map_send.at[peer, piece])

    def down_maps(act):
        for gap in range(reach, 0, -1):
            for piece in range(pieces):
                @pl.when(me_c >= gap)
                def _():
                    act(own_copy(me_c - gap, piece))

    def up_maps(act, wait):
        for gap in range(reach, 0, -1):
            @pl.when(me_c + gap < m)
            def _():
                if wait:
                    pl.semaphore_wait(entered.at[me_c + gap], 1)
                for piece in range(pieces):
                    act(own_copy(me_c + gap, piece))

    def relay_copy(peer, slot, piece):
        return map_copy(peer, slot, piece, relay_send.at[piece])

    def relay(first, last):
        if relayed:
            for piece in range(first, min(last, pieces)):
                @pl.when(me_c == 1)
                def _():
                    relay_copy(1, m - 1, piece).wait_recv()
                    relay_copy(0, m - 1, piece).start()

                @pl.when(me_c == m - 2)
                def _():
                    relay_copy(m - 2, 0, piece).wait_recv()
                    relay_copy(m - 1, 0, piece).start()

    def relay_done():
        if relayed:
            for piece in range(pieces):
                @pl.when(me_c == 1)
                def _():
                    relay_copy(0, m - 1, piece).wait_send()

                @pl.when(me_c == m - 2)
                def _():
                    relay_copy(m - 1, 0, piece).wait_send()

    def maps_wait():
        for j in range(m):
            early = (me_c == 1) & (j == m - 1) | (me_c == m - 2) & (j == 0) if relayed else me_c < 0

            @pl.when((j != me_c) & jnp.logical_not(early))
            def _():
                for piece in range(pieces):
                    relay_copy(me_c, j, piece).wait_recv()

    def part_copy(it, peer, slot):
        return pltpu.make_async_remote_copy(
            src_ref=part_out.at[it, pl.ds(peer, 3)], dst_ref=part_in.at[it, slot],
            send_sem=part_send.at[it, peer], recv_sem=part_recv.at[it, slot],
            device_id={"sub": peer}, device_id_type=MESH)

    get_state.wait()
    sent[0] = cur[...].astype(BF16)
    get_map.wait()
    mine = own[...]
    mine = jnp.concatenate([mine, mine[nc - TAIL :]], axis=0)
    maps[me_c] = fold(dot_nt(diagonal(n * per), mine), full).astype(BF16)

    pl.semaphore_wait(barrier, n - 1 + lax.min(me_c, reach))
    outward(halo_copy, 0, begin)
    down_maps(begin)
    for gap in range(1, reach + 1):
        @pl.when(me_c >= gap)
        def _():
            pl.semaphore_signal(entered.at[me_c], inc=1, device_id={"col": me_c - gap}, device_id_type=MESH)

    def stack(s):
        def gather(at, low, high):
            found = []
            for a in range(low // per, -(-high // per)):
                first, last = max(low - a * per, 0), min(high - a * per, per)
                found.append(maps[a, at + s * per + first : at + s * per + last, :])
            if per % 16:
                return jnp.concatenate([piece.astype(F32) for piece in found], axis=0).astype(BF16)
            return jnp.concatenate(found, axis=0)

        def block(at):
            whole = gather(at, 0, nc)
            return jnp.concatenate([whole, whole[nc - TAIL :]], axis=0)

        tail_at = full * n * per - (n // 2 * per if s >= n // 2 else 0)
        return jnp.concatenate([block(f * n * per) for f in range(full)] + [block(tail_at)], axis=1)

    def partials(it, rb):
        wide = dot_nt(rb, basis[...])
        lane = lanes_of(wide)
        low = jnp.where(lane < nc, wide, 0.0).astype(BF16)
        high = jnp.where((lane < full * LANES) | (lane >= nc), wide, 0.0).astype(BF16)
        for s in range(n):
            part_out[it, s + 1] = fold(dot_nt(low if s < n // 2 else high, stack(s)), full).astype(BF16)
        for k in sorted(range(1, n), key=lambda k: -min(k, n - k)):
            part_copy(it, lax.rem(me_s + k, n), me_s).start()
        part_in[it, me_s] = part_out[it, pl.ds(me_s, 3)]

    def coarse(it):
        for k in range(1, n):
            part_copy(it, me_s, lax.rem(me_s + k, n)).wait_recv()
        total = part_in[it, 0].astype(F32)
        for s in range(1, n):
            total = total + part_in[it, s].astype(F32)
        total = [unfold(total[i], rows, full).astype(BF16) for i in range(3)]
        return dot(total[1], basis[...]), dot(jnp.concatenate(total, axis=1), lifted[...])

    def lift_operator():
        def put(i, value):
            tall = nc + TAIL
            value = value.astype(BF16)
            lifted[i * tall : i * tall + nc, :] = value
            lifted[i * tall + nc : (i + 1) * tall, :] = value[nc - TAIL :]

        put(1, dot(basis[:nc], diag[...]))
        inward(near_copy, 0)
        put(0, dot(near[0], rim[:h]))
        put(2, dot(near[1], rim[h:]))

    def permuted_inverse():
        used = ov[...]
        slot = lax.broadcasted_iota(jnp.int32, used.shape, 1)
        used = jnp.where(slot < count[0], used, -1)
        chunk = 2 * h // 4
        for i in range(4):
            place = lax.broadcasted_iota(jnp.int32, (chunk, slots), 0) + i * chunk
            pick = (place == used).astype(F32).astype(BF16)
            invp[i * chunk : (i + 1) * chunk, :] = dot(pick, inv[half:, :]).astype(BF16)
            if i > 0:
                relay(i - 1, i)

    get_diag.wait()
    acc = dot(sent[0], diag[...])
    up_maps(begin, True)
    get_basis.wait()
    get_again.wait()
    outward(near_copy, 0, begin)
    get_rim.wait()
    inward(halo_copy, 0)
    acc = acc + dot(halo[0, 0], rim[:h]) + dot(halo[0, 1], rim[h:])
    get_load.wait()

    for it in range(ITERS):
        first = it == 0
        v = cur[...]
        rb = (load[...] - acc - cubic_coef * v * v * v).astype(BF16)
        e = 2 * it + 1
        sent[e] = rb
        outward(halo_copy, e, begin)
        if first:
            get_inv.wait()
            get_ov.wait()
            get_count.wait()
            permuted_inverse()
        else:
            partials(it, rb)
        fine = dot(rb, inv[:half, :])
        inward(halo_copy, e)
        v = v + (fine + dot(halo[e, 0], invp[:h, :]) + dot(halo[e, 1], invp[h:, :]))
        e = e + 1
        sent[e] = v.astype(BF16)
        outward(halo_copy, e, begin)
        acc = dot(sent[e], diag[...])
        if first:
            relay(3, pieces)
            lift_operator()
            maps_wait()
            partials(it, rb)
        inward(halo_copy, e)
        acc = acc + dot(halo[e, 0], rim[:h]) + dot(halo[e, 1], rim[h:])
        lift, spread = coarse(it)
        acc = acc + spread
        if it < ITERS - 1:
            cur[...] = v + lift
        else:
            before_ref[...] = v
            change_ref[...] = lift
    applied_ref[...] = acc

    for e in range(2 * ITERS + 1):
        outward(halo_copy, e, finish)
    outward(near_copy, 0, finish)
    down_maps(finish)
    up_maps(finish, False)
    relay_done()
    for it in range(ITERS):
        for k in range(1, n):
            part_copy(it, lax.rem(me_s + k, n), me_s).wait_send()


def body(n, m, state_init, load_cols, stiff_diag, stiff_rim, inverse, ov_rows, ov_count, coarse_basis, coarse_map):
    rows, width = state_init.shape
    h = stiff_rim.shape[0] // 2
    basis_t = coarse_basis.T
    nc = basis_t.shape[0]
    if nc % LANES != TAIL or n % 2 or rows % 32:
        raise ValueError("unsupported sizes")
    full = nc // LANES
    trades = 2 * ITERS + 1
    packed = (rows * full + rows // 2, LANES)
    hbm = pl.BlockSpec(memory_space=pltpu.HBM)
    vmem = pl.BlockSpec(memory_space=pltpu.VMEM)
    dma = pltpu.SemaphoreType.DMA
    out = jax.ShapeDtypeStruct((rows, width), F32)
    before, change, product = pl.pallas_call(
        functools.partial(kernel, n, m),
        out_shape=(out, out, out),
        in_specs=[hbm] * 9,
        out_specs=(vmem, vmem, vmem),
        scratch_shapes=[
            pltpu.VMEM((rows, width), F32),
            pltpu.VMEM((rows, width), F32),
            pltpu.VMEM(stiff_diag.shape, BF16),
            pltpu.VMEM(stiff_rim.shape, BF16),
            pltpu.VMEM(inverse.shape, BF16),
            pltpu.VMEM(ov_rows.shape, jnp.int32),
            pltpu.SMEM((1,), jnp.int32),
            pltpu.VMEM((nc + TAIL, width), BF16),
            pltpu.VMEM((2, nc, h), BF16),
            pltpu.VMEM((3 * (nc + TAIL), width), BF16),
            pltpu.VMEM(coarse_map.shape, BF16),
            pltpu.VMEM((m, coarse_map.shape[1] * full + coarse_map.shape[1] // 2, LANES), BF16),
            pltpu.VMEM((2 * h, width), BF16),
            pltpu.VMEM((trades, rows, width), BF16),
            pltpu.VMEM((trades, 2, rows, h), BF16),
            pltpu.VMEM((ITERS, n + 2) + packed, BF16),
            pltpu.VMEM((ITERS, n, 3) + packed, BF16),
            dma((10,)),
            dma((trades, 2)),
            dma((trades, 2)),
            dma((2,)),
            dma((2,)),
            dma((m, PIECES)),
            dma((m, PIECES)),
            dma((PIECES,)),
            dma((ITERS, n)),
            dma((ITERS, n)),
            pltpu.SemaphoreType.REGULAR((m,)),
        ],
        compiler_params=pltpu.CompilerParams(collective_id=0, has_side_effects=True, vmem_limit_bytes=40 * 2**20),
        name="schwarz",
    )(state_init, load_cols, stiff_diag, stiff_rim, inverse, ov_rows, ov_count, basis_t, coarse_map)
    current = before + change
    return current, load_cols - product - cubic_coef * current * current * current


def solution(mesh):
    in_specs = (
        P("col", "sub"),
        P("col", "sub"),
        P(None, "sub"),
        P(None, "sub"),
        P(None, "sub"),
        P("sub", None),
        P("sub"),
        P("sub", None),
        P("sub", "col"),
    )
    out_specs = (P("col", "sub"), P("col", "sub"))
    step = functools.partial(body, mesh.shape["sub"], mesh.shape["col"])
    return jax.shard_map(step, mesh=mesh, in_specs=in_specs, out_specs=out_specs, check_vma=False)
```

```python
import functools

import jax
import jax.numpy as jnp
from jax import lax
from jax.experimental import pallas as pl
from jax.experimental.pallas import tpu as pltpu
from jax.sharding import PartitionSpec as P

ITERS = 2
PIECES = 4

cubic_coef = 0.1
MESH = pl.DeviceIdType.MESH
F32 = jnp.float32
BF16 = jnp.bfloat16


NEAR, FAR = 0, 1
TAIL = 64
LANES = 128


def dot(a, b):
    return jnp.dot(a, b, preferred_element_type=F32)


def dot_nt(a, b):
    return lax.dot_general(a, b, (((1,), (1,)), ((), ())), preferred_element_type=F32)


def diagonal(size):
    place = [lax.broadcasted_iota(jnp.int32, (size, size), axis) for axis in (0, 1)]
    return (place[0] == place[1]).astype(F32).astype(BF16)


def lanes_of(value):
    return lax.broadcasted_iota(jnp.int32, value.shape, 1)


def fold(wide, full):
    half = wide.shape[0] // 2
    tail = wide[:, full * LANES :]
    low = lanes_of(tail[:half]) < TAIL
    tail = jnp.where(low, tail[:half], tail[half:])
    return jnp.concatenate([wide[:, f * LANES : (f + 1) * LANES] for f in range(full)] + [tail], axis=0)


def unfold(packed, rows, full):
    tail = packed[rows * full :]
    tail = jnp.concatenate([tail, tail], axis=0)
    upper = lax.broadcasted_iota(jnp.int32, tail.shape, 0) < rows // 2
    tail = jnp.where(upper == (lanes_of(tail) < TAIL), tail, jnp.zeros_like(tail))
    return jnp.concatenate([packed[f * rows : (f + 1) * rows] for f in range(full)] + [tail], axis=1)


def kernel(
    n, m,
    state_hbm, load_hbm, diag_hbm, rim_hbm, inv_hbm, ov_hbm, count_hbm, basis_hbm, map_hbm,
    before_ref, change_ref, applied_ref,
    cur, load, base, diag, rim, inv, ov, count, basis, near, lifted, own, maps, invp,
    sent, halo, part_out, part_in,
    local_sem, halo_send, halo_recv, near_send, near_recv, map_send, map_recv, relay_send, part_send, part_recv, entered,
):
    me_s = lax.axis_index("sub")
    me_c = lax.axis_index("col")
    rows, width = cur.shape
    h = halo.shape[3]
    nc = near.shape[1]
    per = nc // m
    full = nc // LANES
    slots = ov.shape[1]
    half = inv.shape[0] - slots
    relayed = m >= 4
    reach = m - 1 - relayed

    barrier = pltpu.get_barrier_semaphore()
    for k in range(1, n):
        pl.semaphore_signal(barrier, inc=1, device_id={"sub": lax.rem(me_s + k, n)}, device_id_type=MESH)
    for gap in range(1, reach + 1):
        @pl.when(me_c + gap < m)
        def _():
            pl.semaphore_signal(barrier, inc=1, device_id={"col": me_c + gap}, device_id_type=MESH)

    def fetch(index, source, target):
        copy = pltpu.make_async_copy(source, target, local_sem.at[index])
        copy.start()
        return copy

    get_state = fetch(0, state_hbm, cur)
    get_map = fetch(1, map_hbm, own)
    get_diag = fetch(2, diag_hbm, diag)
    get_basis = fetch(3, basis_hbm, basis.at[pl.ds(0, nc)])
    get_again = fetch(4, basis_hbm.at[pl.ds(nc - TAIL, TAIL)], basis.at[pl.ds(nc, TAIL)])
    get_rim = fetch(5, rim_hbm, rim)
    get_load = fetch(6, load_hbm, load)
    get_ov = fetch(7, ov_hbm, ov)
    get_count = fetch(8, count_hbm, count)
    get_inv = fetch(9, inv_hbm, inv)

    odd = lax.rem(me_s, 2)
    has_far = (me_s > 0) & (me_s < n - 1)
    towards = (lax.rem(me_s + n + 1 - 2 * odd, n), lax.rem(me_s + n - 1 + 2 * odd, n))
    part = tuple(pl.ds(pl.multiple_of(at, h), h) for at in ((1 - odd) * h, odd * h))

    @pl.when(jnp.logical_not(has_far))
    def _():
        near[FAR] = jnp.zeros(near.shape[1:], BF16)
        for e in range(2 * ITERS + 1):
            halo[e, FAR] = jnp.zeros((rows, h), BF16)

    for it in range(ITERS):
        for edge in (0, n + 1):
            part_out[it, edge] = jnp.zeros(part_out.shape[2:], BF16)

    def trade(source, target, send, recv, side):
        return pltpu.make_async_remote_copy(
            src_ref=source, dst_ref=target, send_sem=send, recv_sem=recv,
            device_id={"sub": towards[side]}, device_id_type=MESH)

    def halo_copy(e, side):
        return trade(
            sent.at[e, :, part[side]], halo.at[e, side], halo_send.at[e, side], halo_recv.at[e, side], side)

    def near_copy(e, side):
        return trade(basis.at[pl.ds(0, nc), part[side]], near.at[side], near_send.at[side], near_recv.at[side], side)

    def only(side, act):
        if side == FAR:
            pl.when(has_far)(act)
        else:
            act()

    def begin(copy, e, side):
        only(side, lambda: copy(e, side).start())

    def arrive(copy, e, side):
        only(side, lambda: copy(e, side).wait_recv())

    def finish(copy, e, side):
        only(side, lambda: copy(e, side).wait_send())

    pieces = PIECES if relayed and maps.shape[1] % (16 * PIECES) == 0 else 1
    tall = maps.shape[1] // pieces

    def map_copy(peer, slot, piece, send):
        block = maps.at[slot, pl.ds(piece * tall, tall), :]
        return pltpu.make_async_remote_copy(
            src_ref=block, dst_ref=block, send_sem=send, recv_sem=map_recv.at[slot, piece],
            device_id={"col": peer}, device_id_type=MESH)

    def own_copy(peer, piece):
        return map_copy(peer, me_c, piece, map_send.at[peer, piece])

    def down_maps(act):
        for gap in range(reach, 0, -1):
            for piece in range(pieces):
                @pl.when(me_c >= gap)
                def _():
                    act(own_copy(me_c - gap, piece))

    def up_maps(act, wait):
        for gap in range(reach, 0, -1):
            @pl.when(me_c + gap < m)
            def _():
                if wait:
                    pl.semaphore_wait(entered.at[me_c + gap], 1)
                for piece in range(pieces):
                    act(own_copy(me_c + gap, piece))

    def relay_copy(peer, slot, piece):
        return map_copy(peer, slot, piece, relay_send.at[piece])

    def relay(first, last):
        if relayed:
            for piece in range(first, min(last, pieces)):
                @pl.when(me_c == 1)
                def _():
                    relay_copy(1, m - 1, piece).wait_recv()
                    relay_copy(0, m - 1, piece).start()

                @pl.when(me_c == m - 2)
                def _():
                    relay_copy(m - 2, 0, piece).wait_recv()
                    relay_copy(m - 1, 0, piece).start()

    def relay_done():
        if relayed:
            for piece in range(pieces):
                @pl.when(me_c == 1)
                def _():
                    relay_copy(0, m - 1, piece).wait_send()

                @pl.when(me_c == m - 2)
                def _():
                    relay_copy(m - 1, 0, piece).wait_send()

    def maps_wait():
        for j in range(m):
            early = (me_c == 1) & (j == m - 1) | (me_c == m - 2) & (j == 0) if relayed else me_c < 0

            @pl.when((j != me_c) & jnp.logical_not(early))
            def _():
                for piece in range(pieces):
                    relay_copy(me_c, j, piece).wait_recv()

    def part_copy(it, peer, slot):
        return pltpu.make_async_remote_copy(
            src_ref=part_out.at[it, pl.ds(peer, 3)], dst_ref=part_in.at[it, slot],
            send_sem=part_send.at[it, peer], recv_sem=part_recv.at[it, slot],
            device_id={"sub": peer}, device_id_type=MESH)

    get_state.wait()
    sent[0] = cur[...].astype(BF16)
    get_map.wait()
    mine = own[...]
    mine = jnp.concatenate([mine, mine[nc - TAIL :]], axis=0)
    maps[me_c] = fold(dot_nt(diagonal(n * per), mine), full).astype(BF16)

    pl.semaphore_wait(barrier, n - 1 + lax.min(me_c, reach))
    begin(halo_copy, 0, FAR)
    begin(halo_copy, 0, NEAR)
    down_maps(lambda copy: copy.start())
    for gap in range(1, reach + 1):
        @pl.when(me_c >= gap)
        def _():
            pl.semaphore_signal(entered.at[me_c], inc=1, device_id={"col": me_c - gap}, device_id_type=MESH)

    def stack(s):
        def gather(at, low, high):
            found = []
            for a in range(low // per, -(-high // per)):
                first, last = max(low - a * per, 0), min(high - a * per, per)
                found.append(maps[a, at + s * per + first : at + s * per + last, :])
            if per % 16:
                return jnp.concatenate([piece.astype(F32) for piece in found], axis=0).astype(BF16)
            return jnp.concatenate(found, axis=0)

        def block(at):
            whole = gather(at, 0, nc)
            return jnp.concatenate([whole, whole[nc - TAIL :]], axis=0)

        tail_at = full * n * per - (n // 2 * per if s >= n // 2 else 0)
        return jnp.concatenate([block(f * n * per) for f in range(full)] + [block(tail_at)], axis=1)

    def partials(it, rb):
        wide = dot_nt(rb, basis[...])
        lane = lanes_of(wide)
        low = jnp.where(lane < nc, wide, 0.0).astype(BF16)
        high = jnp.where((lane < full * LANES) | (lane >= nc), wide, 0.0).astype(BF16)
        for s in range(n):
            part_out[it, s + 1] = fold(dot_nt(low if s < n // 2 else high, stack(s)), full).astype(BF16)
        for k in sorted(range(1, n), key=lambda k: -min(k, n - k)):
            part_copy(it, lax.rem(me_s + k, n), me_s).start()
        part_in[it, me_s] = part_out[it, pl.ds(me_s, 3)]

    def coarse(it):
        for k in range(1, n):
            part_copy(it, me_s, lax.rem(me_s + k, n)).wait_recv()
        total = part_in[it, 0].astype(F32)
        for s in range(1, n):
            total = total + part_in[it, s].astype(F32)
        total = [unfold(total[i], rows, full).astype(BF16) for i in range(3)]
        return total[1], jnp.concatenate(total, axis=1)

    def lift_operator():
        deep = nc + TAIL

        def put(i, value):
            value = value.astype(BF16)
            value = jnp.concatenate([value, value[nc - TAIL :]], axis=0)
            lifted[pl.ds(pl.multiple_of(i * deep, deep), deep), :] = value

        put(1, dot(basis[:nc], diag[...]))
        for side, i in ((NEAR, 2 * (1 - odd)), (FAR, 2 * odd)):
            arrive(near_copy, 0, side)
            put(i, dot(near[side], rim[part[side], :]))

    def permuted_inverse():
        used = ov[...]
        slot = lax.broadcasted_iota(jnp.int32, used.shape, 1)
        used = jnp.where(slot < count[...], used, -1)
        chunk = 2 * h // 4
        for i in range(4):
            place = lax.broadcasted_iota(jnp.int32, (chunk, slots), 0) + i * chunk
            pick = (place == used).astype(F32).astype(BF16)
            invp[i * chunk : (i + 1) * chunk, :] = dot(pick, inv[half:, :]).astype(BF16)
            if i > 0:
                relay(i - 1, i)

    def own_and_near(e, weights, margin):
        base[...] = dot(sent[e], weights)
        arrive(halo_copy, e, NEAR)
        base[...] += dot(halo[e, NEAR], margin[part[NEAR], :])

    def far_part(e, margin, columns):
        return dot(halo[e, FAR], margin[part[FAR], columns])

    def residual(e, columns, product):
        v = cur[:, columns]
        sent[e, :, columns] = (load[:, columns] - product - cubic_coef * v * v * v).astype(BF16)

    get_diag.wait()
    base[...] = dot(sent[0], diag[...])
    up_maps(lambda copy: copy.start(), True)
    get_basis.wait()
    get_again.wait()
    begin(near_copy, 0, FAR)
    begin(near_copy, 0, NEAR)
    get_rim.wait()
    arrive(halo_copy, 0, NEAR)
    base[...] += dot(halo[0, NEAR], rim[part[NEAR], :])
    get_load.wait()
    arrive(halo_copy, 0, FAR)
    for side in (FAR, NEAR):
        residual(1, part[side], base[:, part[side]] + far_part(0, rim, part[side]))
        begin(halo_copy, 1, side)

    for it in range(ITERS):
        first, last = it == 0, it == ITERS - 1
        e = 2 * it + 1
        if first:
            get_inv.wait()
            get_ov.wait()
            get_count.wait()
            permuted_inverse()
        else:
            partials(it, sent[e])
        own_and_near(e, inv[:half, :], invp)
        arrive(halo_copy, e, FAR)
        for side in (FAR, NEAR):
            v = cur[:, part[side]] + (base[:, part[side]] + far_part(e, invp, part[side]))
            cur[:, part[side]] = v
            sent[e + 1, :, part[side]] = v.astype(BF16)
            begin(halo_copy, e + 1, side)
        if first:
            relay(3, pieces)
            lift_operator()
            maps_wait()
            partials(it, sent[e])
        e = e + 1
        own_and_near(e, diag[...], rim)
        if first:
            arrive(halo_copy, e, FAR)
            base[...] += far_part(e, rim, slice(None))
        mine, three = coarse(it)
        if last:
            before_ref[...] = cur[...]
            change_ref[...] = dot(mine, basis[...])
            base[...] += dot(three, lifted[...])
            if not first:
                arrive(halo_copy, e, FAR)
                base[...] += far_part(e, rim, slice(None))
            applied_ref[...] = base[...]
        elif first:
            for side in (FAR, NEAR):
                cur[:, part[side]] += dot(mine, basis[:, part[side]])
                residual(e + 1, part[side], base[:, part[side]] + dot(three, lifted[:, part[side]]))
                begin(halo_copy, e + 1, side)
        else:
            cur[...] += dot(mine, basis[...])
            base[...] += dot(three, lifted[...])
            arrive(halo_copy, e, FAR)
            for side in (FAR, NEAR):
                residual(e + 1, part[side], base[:, part[side]] + far_part(e, rim, part[side]))
                begin(halo_copy, e + 1, side)

    for side in (FAR, NEAR):
        for e in range(2 * ITERS + 1):
            finish(halo_copy, e, side)
        finish(near_copy, 0, side)
    down_maps(lambda copy: copy.wait_send())
    up_maps(lambda copy: copy.wait_send(), False)
    relay_done()
    for it in range(ITERS):
        for k in range(1, n):
            part_copy(it, lax.rem(me_s + k, n), me_s).wait_send()


def body(n, m, state_init, load_cols, stiff_diag, stiff_rim, inverse, ov_rows, ov_count, coarse_basis, coarse_map):
    rows, width = state_init.shape
    h = stiff_rim.shape[0] // 2
    basis_t = coarse_basis.T
    nc = basis_t.shape[0]
    if nc % LANES != TAIL or n % 2 or rows % 32 or width != 2 * h:
        raise ValueError("unsupported sizes")
    full = nc // LANES
    trades = 2 * ITERS + 1
    packed = (rows * full + rows // 2, LANES)
    hbm = pl.BlockSpec(memory_space=pltpu.HBM)
    vmem = pl.BlockSpec(memory_space=pltpu.VMEM)
    dma = pltpu.SemaphoreType.DMA
    out = jax.ShapeDtypeStruct((rows, width), F32)
    before, change, product = pl.pallas_call(
        functools.partial(kernel, n, m),
        out_shape=(out, out, out),
        in_specs=[hbm] * 9,
        out_specs=(vmem, vmem, vmem),
        scratch_shapes=[
            pltpu.VMEM((rows, width), F32),
            pltpu.VMEM((rows, width), F32),
            pltpu.VMEM((rows, width), F32),
            pltpu.VMEM(stiff_diag.shape, BF16),
            pltpu.VMEM(stiff_rim.shape, BF16),
            pltpu.VMEM(inverse.shape, BF16),
            pltpu.VMEM(ov_rows.shape, jnp.int32),
            pltpu.VMEM((1, 1), jnp.int32),
            pltpu.VMEM((nc + TAIL, width), BF16),
            pltpu.VMEM((2, nc, h), BF16),
            pltpu.VMEM((3 * (nc + TAIL), width), BF16),
            pltpu.VMEM(coarse_map.shape, BF16),
            pltpu.VMEM((m, coarse_map.shape[1] * full + coarse_map.shape[1] // 2, LANES), BF16),
            pltpu.VMEM((2 * h, width), BF16),
            pltpu.VMEM((trades, rows, width), BF16),
            pltpu.VMEM((trades, 2, rows, h), BF16),
            pltpu.VMEM((ITERS, n + 2) + packed, BF16),
            pltpu.VMEM((ITERS, n, 3) + packed, BF16),
            dma((10,)),
            dma((trades, 2)),
            dma((trades, 2)),
            dma((2,)),
            dma((2,)),
            dma((m, PIECES)),
            dma((m, PIECES)),
            dma((PIECES,)),
            dma((ITERS, n)),
            dma((ITERS, n)),
            pltpu.SemaphoreType.REGULAR((m,)),
        ],
        compiler_params=pltpu.CompilerParams(collective_id=0, has_side_effects=True, vmem_limit_bytes=60 * 2**20),
        name="schwarz",
    )(state_init, load_cols, stiff_diag, stiff_rim, inverse, ov_rows, ov_count.reshape(1, 1), basis_t, coarse_map)
    current = before + change
    return current, load_cols - product - cubic_coef * current * current * current


def solution(mesh):
    in_specs = (
        P("col", "sub"),
        P("col", "sub"),
        P(None, "sub"),
        P(None, "sub"),
        P(None, "sub"),
        P("sub", None),
        P("sub"),
        P("sub", None),
        P("sub", "col"),
    )
    out_specs = (P("col", "sub"), P("col", "sub"))
    step = functools.partial(body, mesh.shape["sub"], mesh.shape["col"])
    return jax.shard_map(step, mesh=mesh, in_specs=in_specs, out_specs=out_specs, check_vma=False)
```

```python
import functools

import jax
import jax.numpy as jnp
from jax import lax
from jax.experimental import pallas as pl
from jax.experimental.pallas import tpu as pltpu
from jax.sharding import PartitionSpec as P

ITERS = 2
PIECES = 4

cubic_coef = 0.1
MESH = pl.DeviceIdType.MESH
F32 = jnp.float32
BF16 = jnp.bfloat16


NEAR, FAR = 0, 1
TAIL = 64
LANES = 128


def dot(a, b):
    return jnp.dot(a, b, preferred_element_type=F32)


def dot_nt(a, b):
    return lax.dot_general(a, b, (((1,), (1,)), ((), ())), preferred_element_type=F32)


def diagonal(size):
    place = [lax.broadcasted_iota(jnp.int32, (size, size), axis) for axis in (0, 1)]
    return (place[0] == place[1]).astype(F32).astype(BF16)


def lanes_of(value):
    return lax.broadcasted_iota(jnp.int32, value.shape, 1)


def fold_tail(tail):
    half = tail.shape[0] // 2
    return jnp.where(lanes_of(tail[:half]) < TAIL, tail[:half], tail[half:])


def fold(wide, full):
    blocks = [wide[:, f * LANES : (f + 1) * LANES] for f in range(full)]
    return jnp.concatenate(blocks + [fold_tail(wide[:, full * LANES :])], axis=0)


def unfold(packed, rows, full):
    tail = packed[rows * full :]
    tail = jnp.concatenate([tail, tail], axis=0)
    upper = lax.broadcasted_iota(jnp.int32, tail.shape, 0) < rows // 2
    tail = jnp.where(upper == (lanes_of(tail) < TAIL), tail, jnp.zeros_like(tail))
    return jnp.concatenate([packed[f * rows : (f + 1) * rows] for f in range(full)] + [tail], axis=1)


def kernel(
    n, m,
    state_hbm, load_hbm, diag_hbm, rim_hbm, inv_hbm, ov_hbm, count_hbm, basis_hbm, map_hbm,
    before_ref, change_ref, applied_ref,
    cur, load, base, diag, rim, inv, ov, count, basis, raised, near, lifted, own, maps, invp,
    sent, halo, part_out, part_in,
    local_sem, halo_send, halo_recv, near_send, near_recv, map_send, map_recv, relay_send, part_send, part_recv, entered,
):
    me_s = lax.axis_index("sub")
    me_c = lax.axis_index("col")
    rows, width = cur.shape
    h = halo.shape[3]
    nc = near.shape[1]
    per = nc // m
    full = nc // LANES
    slots = ov.shape[1]
    half = inv.shape[0] - slots
    deep = nc + TAIL
    relayed = m >= 4
    reach = m - 1 - relayed

    barrier = pltpu.get_barrier_semaphore()
    for k in range(1, n):
        pl.semaphore_signal(barrier, inc=1, device_id={"sub": lax.rem(me_s + k, n)}, device_id_type=MESH)
    for gap in range(1, reach + 1):
        @pl.when(me_c + gap < m)
        def _():
            pl.semaphore_signal(barrier, inc=1, device_id={"col": me_c + gap}, device_id_type=MESH)

    def fetch(index, source, target):
        copy = pltpu.make_async_copy(source, target, local_sem.at[index])
        copy.start()
        return copy

    get_state = fetch(0, state_hbm, cur)
    get_map = fetch(1, map_hbm, own)
    get_diag = fetch(2, diag_hbm, diag)
    get_basis = fetch(3, basis_hbm, basis.at[pl.ds(0, nc)])
    get_again = fetch(4, basis_hbm.at[pl.ds(nc - TAIL, TAIL)], basis.at[pl.ds(nc, TAIL)])
    get_rim = fetch(5, rim_hbm, rim)
    get_load = fetch(6, load_hbm, load)
    get_ov = fetch(7, ov_hbm, ov)
    get_count = fetch(8, count_hbm, count)
    get_inv = fetch(9, inv_hbm, inv)

    odd = lax.rem(me_s, 2)
    has_far = (me_s > 0) & (me_s < n - 1)
    towards = (lax.rem(me_s + n + 1 - 2 * odd, n), lax.rem(me_s + n - 1 + 2 * odd, n))
    part = tuple(pl.ds(pl.multiple_of(at, h), h) for at in ((1 - odd) * h, odd * h))

    @pl.when(jnp.logical_not(has_far))
    def _():
        near[FAR] = jnp.zeros(near.shape[1:], BF16)
        for e in range(2 * ITERS + 1):
            halo[e, FAR] = jnp.zeros((rows, h), BF16)

    for it in range(ITERS):
        for edge in (0, n + 1):
            part_out[it, edge] = jnp.zeros(part_out.shape[2:], BF16)

    def trade(source, target, send, recv, side):
        return pltpu.make_async_remote_copy(
            src_ref=source, dst_ref=target, send_sem=send, recv_sem=recv,
            device_id={"sub": towards[side]}, device_id_type=MESH)

    def halo_copy(e, side):
        return trade(
            sent.at[e, :, part[side]], halo.at[e, side], halo_send.at[e, side], halo_recv.at[e, side], side)

    def near_copy(e, side):
        return trade(basis.at[pl.ds(0, nc), part[side]], near.at[side], near_send.at[side], near_recv.at[side], side)

    def only(side, act):
        if side == FAR:
            pl.when(has_far)(act)
        else:
            act()

    def begin(copy, e, side):
        only(side, lambda: copy(e, side).start())

    def arrive(copy, e, side):
        only(side, lambda: copy(e, side).wait_recv())

    def finish(copy, e, side):
        only(side, lambda: copy(e, side).wait_send())

    pieces = PIECES if relayed and maps.shape[1] % (16 * PIECES) == 0 else 1
    tall = maps.shape[1] // pieces

    def map_copy(peer, slot, piece, send):
        block = maps.at[slot, pl.ds(piece * tall, tall), :]
        return pltpu.make_async_remote_copy(
            src_ref=block, dst_ref=block, send_sem=send, recv_sem=map_recv.at[slot, piece],
            device_id={"col": peer}, device_id_type=MESH)

    def own_copy(peer, piece):
        return map_copy(peer, me_c, piece, map_send.at[peer, piece])

    def down_maps(act):
        for gap in range(reach, 0, -1):
            for piece in range(pieces):
                @pl.when(me_c >= gap)
                def _():
                    act(own_copy(me_c - gap, piece))

    def up_maps(act, wait):
        for gap in range(reach, 0, -1):
            @pl.when(me_c + gap < m)
            def _():
                if wait:
                    pl.semaphore_wait(entered.at[me_c + gap], 1)
                for piece in range(pieces):
                    act(own_copy(me_c + gap, piece))

    def relay_copy(peer, slot, piece):
        return map_copy(peer, slot, piece, relay_send.at[piece])

    def relay(first, last):
        if relayed:
            for piece in range(first, min(last, pieces)):
                @pl.when(me_c == 1)
                def _():
                    relay_copy(1, m - 1, piece).wait_recv()
                    relay_copy(0, m - 1, piece).start()

                @pl.when(me_c == m - 2)
                def _():
                    relay_copy(m - 2, 0, piece).wait_recv()
                    relay_copy(m - 1, 0, piece).start()

    def relay_done():
        if relayed:
            for piece in range(pieces):
                @pl.when(me_c == 1)
                def _():
                    relay_copy(0, m - 1, piece).wait_send()

                @pl.when(me_c == m - 2)
                def _():
                    relay_copy(m - 1, 0, piece).wait_send()

    upper = me_c < m // 2
    shift = ((me_c == 1) | (me_c == m - 2)).astype(jnp.int32) if relayed else 0
    turns = [lax.rem(i - shift + m, m) for i in range(m)]
    order = [jnp.where(upper, turn, m - 1 - turn) for turn in turns]
    early = -(-full * LANES // per)

    def maps_wait(first, last):
        for j in order[first:last]:
            known = (me_c == 1) & (j == m - 1) | (me_c == m - 2) & (j == 0) if relayed else me_c < 0

            @pl.when((j != me_c) & jnp.logical_not(known))
            def _():
                for piece in range(pieces):
                    relay_copy(me_c, j, piece).wait_recv()

    mains = rows * full

    def part_copy(it, peer, slot, kind):
        if kind < 2:
            lines = (pl.ds(0, mains), pl.ds(mains, rows // 2))[kind]
            source, target = part_out.at[it, pl.ds(peer, 3), lines], part_in.at[it, slot, :, lines]
        else:
            source, target = part_out.at[it, pl.ds(peer + lax.rem(peer, 2), 2)], part_in.at[it, slot, pl.ds(0, 2)]
        return pltpu.make_async_remote_copy(
            src_ref=source, dst_ref=target,
            send_sem=part_send.at[it, kind % 2, peer], recv_sem=part_recv.at[it, kind % 2, slot],
            device_id={"sub": peer}, device_id_type=MESH)

    def part_start(it, kind):
        for k in sorted(range(1, n), key=lambda k: -min(k, n - k)):
            part_copy(it, lax.rem(me_s + k, n), me_s, kind).start()

    def part_wait(it, kind):
        for k in range(1, n):
            part_copy(it, me_s, lax.rem(me_s + k, n), kind).wait_recv()

    get_state.wait()
    sent[0] = cur[...].astype(BF16)
    get_map.wait()
    mine = own[...]
    mine = jnp.concatenate([mine, mine[nc - TAIL :]], axis=0)
    maps[me_c] = fold(dot_nt(diagonal(n * per), mine), full).astype(BF16)

    pl.semaphore_wait(barrier, n - 1 + lax.min(me_c, reach))
    begin(halo_copy, 0, FAR)
    begin(halo_copy, 0, NEAR)
    down_maps(lambda copy: copy.start())
    for gap in range(1, reach + 1):
        @pl.when(me_c >= gap)
        def _():
            pl.semaphore_signal(entered.at[me_c], inc=1, device_id={"col": me_c - gap}, device_id_type=MESH)

    def stack(s, low, high):
        def gather(at):
            found = []
            for i in range(low // per, -(-high // per)):
                first, last = max(low - i * per, 0), min(high - i * per, per)
                found.append(maps[order[i], at + s * per + first : at + s * per + last, :])
            if per % 16:
                return jnp.concatenate([piece.astype(F32) for piece in found], axis=0).astype(BF16)
            return jnp.concatenate(found, axis=0)

        tail_at = full * n * per - (n // 2 * per if s >= n // 2 else 0)
        return jnp.concatenate([gather(f * n * per) for f in range(full)] + [gather(tail_at)], axis=1)

    def coefficients(rb):
        wide = dot_nt(rb, basis[...])
        lane = lanes_of(wide)
        low = jnp.where(lane < nc, wide, 0.0).astype(BF16)
        high = jnp.where((lane < full * LANES) | (lane >= nc), wide, 0.0).astype(BF16)
        return low, high

    def main_parts(it, sides):
        for s in range(n):
            wide = dot_nt(sides[s >= n // 2], stack(s, 0, full * LANES))
            wide = jnp.concatenate([wide[:, f * LANES : (f + 1) * LANES] for f in range(full)], axis=0)
            part_out[it, s + 1, pl.ds(0, mains)] = wide.astype(BF16)

    def tail_parts(it, sides):
        for s in range(n):
            block = stack(s, nc - TAIL, nc)
            tail = dot_nt(sides[s >= n // 2], jnp.concatenate([block, block], axis=0))
            part_out[it, s + 1, pl.ds(mains, rows // 2)] = fold_tail(tail).astype(BF16)

    def whole_parts(it, sides):
        for s in range(n):
            block = stack(s, 0, nc)
            wide = dot_nt(sides[s >= n // 2], jnp.concatenate([block, block[nc - TAIL :]], axis=0))
            part_out[it, s + 1] = fold(wide, full).astype(BF16)

    def coarse(it, count):
        total = part_in[it, 0, 0:count].astype(F32)
        for s in range(1, n):
            total = total + part_in[it, s, 0:count].astype(F32)
        return [unfold(total[i], rows, full).astype(BF16) for i in range(count)]

    def lift_operator():
        row = lax.broadcasted_iota(jnp.int32, (deep, nc), 0)
        row = jnp.where(row < nc, row, row - TAIL)
        source = row
        for i in range(m):
            here = (row >= i * per) & (row < (i + 1) * per)
            source = jnp.where(here, row + (order[i] - i) * per, source)
        place = (lax.broadcasted_iota(jnp.int32, (deep, nc), 1) == source).astype(F32).astype(BF16)

        def put(i, value):
            value = dot(place, value.astype(BF16)).astype(BF16)
            lifted[pl.ds(pl.multiple_of(i * deep, deep), deep), :] = value

        raised[...] = dot(place, basis[:nc]).astype(BF16)
        put(1, dot(basis[:nc], diag[...]))
        for side, i in ((NEAR, 2 * (1 - odd)), (FAR, 2 * odd)):
            arrive(near_copy, 0, side)
            put(i, dot(near[side], rim[part[side], :]))

    def permuted_inverse():
        used = ov[...]
        slot = lax.broadcasted_iota(jnp.int32, used.shape, 1)
        used = jnp.where(slot < count[...], used, -1)
        chunk = 2 * h // 4
        for i in range(4):
            place = lax.broadcasted_iota(jnp.int32, (chunk, slots), 0) + i * chunk
            pick = (place == used).astype(F32).astype(BF16)
            invp[i * chunk : (i + 1) * chunk, :] = dot(pick, inv[half:, :]).astype(BF16)
            if i > 0:
                relay(i - 1, i)

    def own_and_near(e, weights, margin):
        base[...] = dot(sent[e], weights)
        arrive(halo_copy, e, NEAR)
        base[...] += dot(halo[e, NEAR], margin[part[NEAR], :])

    def far_part(e, margin, columns):
        return dot(halo[e, FAR], margin[part[FAR], columns])

    def residual(e, columns, product):
        v = cur[:, columns]
        sent[e, :, columns] = (load[:, columns] - product - cubic_coef * v * v * v).astype(BF16)

    get_diag.wait()
    base[...] = dot(sent[0], diag[...])
    up_maps(lambda copy: copy.start(), True)
    get_basis.wait()
    get_again.wait()
    begin(near_copy, 0, FAR)
    begin(near_copy, 0, NEAR)
    get_rim.wait()
    arrive(halo_copy, 0, NEAR)
    base[...] += dot(halo[0, NEAR], rim[part[NEAR], :])
    get_load.wait()
    arrive(halo_copy, 0, FAR)
    for side in (FAR, NEAR):
        residual(1, part[side], base[:, part[side]] + far_part(0, rim, part[side]))
        begin(halo_copy, 1, side)

    for it in range(ITERS):
        first, last = it == 0, it == ITERS - 1
        e = 2 * it + 1
        if first:
            get_inv.wait()
            get_ov.wait()
            get_count.wait()
            permuted_inverse()
        else:
            whole_parts(it, coefficients(sent[e]))
            part_start(it, 2)
            part_in[it, me_s, 0:2] = part_out[it, pl.ds(me_s + odd, 2)]
        own_and_near(e, inv[:half, :], invp)
        arrive(halo_copy, e, FAR)
        for side in (FAR, NEAR):
            v = cur[:, part[side]] + (base[:, part[side]] + far_part(e, invp, part[side]))
            cur[:, part[side]] = v
            sent[e + 1, :, part[side]] = v.astype(BF16)
            if first or side == FAR:
                begin(halo_copy, e + 1, side)
        if first:
            relay(3, pieces)
            sides = coefficients(sent[e])
            maps_wait(0, early)
            main_parts(it, sides)
            part_start(it, 0)
            lift_operator()
            own_and_near(e + 1, diag[...], rim)
            maps_wait(early, m)
            tail_parts(it, sides)
            part_start(it, 1)
            part_in[it, me_s] = part_out[it, pl.ds(me_s, 3)]
            e = e + 1
            arrive(halo_copy, e, FAR)
            base[...] += far_part(e, rim, slice(None))
            part_wait(it, 0)
            part_wait(it, 1)
            three = coarse(it, 3)
            mine, three = three[1], jnp.concatenate(three, axis=1)
            for side in (FAR, NEAR):
                cur[:, part[side]] += dot(mine, raised[:, part[side]])
                residual(e + 1, part[side], base[:, part[side]] + dot(three, lifted[:, part[side]]))
                begin(halo_copy, e + 1, side)
        else:
            e = e + 1
            base[...] = dot(sent[e], diag[...])
            part_wait(it, 2)
            pair = coarse(it, 2)
            mine = jnp.where(odd == 1, pair[0].astype(F32), pair[1].astype(F32)).astype(BF16)
            change = dot(mine, raised[...])
            if last:
                before_ref[...] = cur[...]
                change_ref[...] = change
            cur[...] += change
            sent[e, :, part[NEAR]] = cur[:, part[NEAR]].astype(BF16)
            begin(halo_copy, e, NEAR)
            both = pl.ds(pl.multiple_of(odd * deep, deep), 2 * deep)
            base[...] += dot(jnp.concatenate(pair, axis=1), lifted[both, :])
            arrive(halo_copy, e, NEAR)
            base[...] += dot(halo[e, NEAR], rim[part[NEAR], :])
            arrive(halo_copy, e, FAR)
            for side in (FAR, NEAR):
                product = base[:, part[side]] + far_part(e, rim, part[side])
                if last:
                    applied_ref[:, part[side]] = product
                else:
                    residual(e + 1, part[side], product)
                    begin(halo_copy, e + 1, side)

    for side in (FAR, NEAR):
        for e in range(2 * ITERS + 1):
            finish(halo_copy, e, side)
        finish(near_copy, 0, side)
    down_maps(lambda copy: copy.wait_send())
    up_maps(lambda copy: copy.wait_send(), False)
    relay_done()
    for it in range(ITERS):
        for kind in (0, 1) if it == 0 else (2,):
            for k in range(1, n):
                part_copy(it, lax.rem(me_s + k, n), me_s, kind).wait_send()


def body(n, m, state_init, load_cols, stiff_diag, stiff_rim, inverse, ov_rows, ov_count, coarse_basis, coarse_map):
    rows, width = state_init.shape
    h = stiff_rim.shape[0] // 2
    basis_t = coarse_basis.T
    nc = basis_t.shape[0]
    if nc % LANES != TAIL or n % 2 or rows % 32 or width != 2 * h:
        raise ValueError("unsupported sizes")
    full = nc // LANES
    trades = 2 * ITERS + 1
    packed = (rows * full + rows // 2, LANES)
    hbm = pl.BlockSpec(memory_space=pltpu.HBM)
    vmem = pl.BlockSpec(memory_space=pltpu.VMEM)
    dma = pltpu.SemaphoreType.DMA
    out = jax.ShapeDtypeStruct((rows, width), F32)
    before, change, product = pl.pallas_call(
        functools.partial(kernel, n, m),
        out_shape=(out, out, out),
        in_specs=[hbm] * 9,
        out_specs=(vmem, vmem, vmem),
        scratch_shapes=[
            pltpu.VMEM((rows, width), F32),
            pltpu.VMEM((rows, width), F32),
            pltpu.VMEM((rows, width), F32),
            pltpu.VMEM(stiff_diag.shape, BF16),
            pltpu.VMEM(stiff_rim.shape, BF16),
            pltpu.VMEM(inverse.shape, BF16),
            pltpu.VMEM(ov_rows.shape, jnp.int32),
            pltpu.VMEM((1, 1), jnp.int32),
            pltpu.VMEM((nc + TAIL, width), BF16),
            pltpu.VMEM((nc + TAIL, width), BF16),
            pltpu.VMEM((2, nc, h), BF16),
            pltpu.VMEM((3 * (nc + TAIL), width), BF16),
            pltpu.VMEM(coarse_map.shape, BF16),
            pltpu.VMEM((m, coarse_map.shape[1] * full + coarse_map.shape[1] // 2, LANES), BF16),
            pltpu.VMEM((2 * h, width), BF16),
            pltpu.VMEM((trades, rows, width), BF16),
            pltpu.VMEM((trades, 2, rows, h), BF16),
            pltpu.VMEM((ITERS, n + 2) + packed, BF16),
            pltpu.VMEM((ITERS, n, 3) + packed, BF16),
            dma((10,)),
            dma((trades, 2)),
            dma((trades, 2)),
            dma((2,)),
            dma((2,)),
            dma((m, PIECES)),
            dma((m, PIECES)),
            dma((PIECES,)),
            dma((ITERS, 2, n)),
            dma((ITERS, 2, n)),
            pltpu.SemaphoreType.REGULAR((m,)),
        ],
        compiler_params=pltpu.CompilerParams(collective_id=0, has_side_effects=True, vmem_limit_bytes=60 * 2**20),
        name="schwarz",
    )(state_init, load_cols, stiff_diag, stiff_rim, inverse, ov_rows, ov_count.reshape(1, 1), basis_t, coarse_map)
    current = before + change
    return current, load_cols - product - cubic_coef * current * current * current


def solution(mesh):
    in_specs = (
        P("col", "sub"),
        P("col", "sub"),
        P(None, "sub"),
        P(None, "sub"),
        P(None, "sub"),
        P("sub", None),
        P("sub"),
        P("sub", None),
        P("sub", "col"),
    )
    out_specs = (P("col", "sub"), P("col", "sub"))
    step = functools.partial(body, mesh.shape["sub"], mesh.shape["col"])
    return jax.shard_map(step, mesh=mesh, in_specs=in_specs, out_specs=out_specs, check_vma=False)
```

```python
import functools

import jax
import jax.numpy as jnp
from jax import lax
from jax.experimental import pallas as pl
from jax.experimental.pallas import tpu as pltpu
from jax.sharding import PartitionSpec as P

ITERS = 2
PIECES = 4

cubic_coef = 0.1
MESH = pl.DeviceIdType.MESH
F32 = jnp.float32
BF16 = jnp.bfloat16


NEAR, FAR = 0, 1
TAIL = 64
LANES = 128


def dot(a, b):
    return jnp.dot(a, b, preferred_element_type=F32)


def dot_nt(a, b):
    return lax.dot_general(a, b, (((1,), (1,)), ((), ())), preferred_element_type=F32)


def diagonal(size):
    place = [lax.broadcasted_iota(jnp.int32, (size, size), axis) for axis in (0, 1)]
    return (place[0] == place[1]).astype(F32).astype(BF16)


def lanes_of(value):
    return lax.broadcasted_iota(jnp.int32, value.shape, 1)


def fold_tail(tail):
    half = tail.shape[0] // 2
    return jnp.where(lanes_of(tail[:half]) < TAIL, tail[:half], tail[half:])


def fold(wide, full):
    blocks = [wide[:, f * LANES : (f + 1) * LANES] for f in range(full)]
    return jnp.concatenate(blocks + [fold_tail(wide[:, full * LANES :])], axis=0)


def unfold(packed, rows, full):
    tail = packed[rows * full :]
    tail = jnp.concatenate([tail, tail], axis=0)
    upper = lax.broadcasted_iota(jnp.int32, tail.shape, 0) < rows // 2
    tail = jnp.where(upper == (lanes_of(tail) < TAIL), tail, jnp.zeros_like(tail))
    return jnp.concatenate([packed[f * rows : (f + 1) * rows] for f in range(full)] + [tail], axis=1)


def kernel(
    n, m,
    state_hbm, load_hbm, diag_hbm, rim_hbm, inv_hbm, ov_hbm, count_hbm, basis_hbm, map_hbm,
    before_ref, change_ref, applied_ref,
    cur, load, base, diag, rim, inv, ov, count, basis, raised, near, lifted, own, maps, invp,
    sent, halo, part_out, part_in,
    local_sem, halo_send, halo_recv, near_send, near_recv, map_send, map_recv, relay_send, part_send, part_recv, entered,
):
    me_s = lax.axis_index("sub")
    me_c = lax.axis_index("col")
    rows, width = cur.shape
    h = halo.shape[3]
    nc = near.shape[1]
    per = nc // m
    full = nc // LANES
    slots = ov.shape[1]
    half = inv.shape[0] - slots
    deep = nc + TAIL
    relayed = m >= 4
    reach = m - 1 - relayed

    barrier = pltpu.get_barrier_semaphore()
    for k in range(1, n):
        pl.semaphore_signal(barrier, inc=1, device_id={"sub": lax.rem(me_s + k, n)}, device_id_type=MESH)
    for gap in range(1, reach + 1):
        @pl.when(me_c + gap < m)
        def _():
            pl.semaphore_signal(barrier, inc=1, device_id={"col": me_c + gap}, device_id_type=MESH)

    def fetch(index, source, target):
        copy = pltpu.make_async_copy(source, target, local_sem.at[index])
        copy.start()
        return copy

    get_state = fetch(0, state_hbm, cur)
    get_map = fetch(1, map_hbm, own)
    get_diag = fetch(2, diag_hbm, diag)
    get_basis = fetch(3, basis_hbm, basis.at[pl.ds(0, nc)])
    get_again = fetch(4, basis_hbm.at[pl.ds(nc - TAIL, TAIL)], basis.at[pl.ds(nc, TAIL)])
    get_rim = fetch(5, rim_hbm, rim)
    get_load = fetch(6, load_hbm, load)
    get_ov = fetch(7, ov_hbm, ov)
    get_count = fetch(8, count_hbm, count)
    get_inv = fetch(9, inv_hbm, inv)

    odd = lax.rem(me_s, 2)
    has_far = (me_s > 0) & (me_s < n - 1)
    towards = (lax.rem(me_s + n + 1 - 2 * odd, n), lax.rem(me_s + n - 1 + 2 * odd, n))
    part = tuple(pl.ds(pl.multiple_of(at, h), h) for at in ((1 - odd) * h, odd * h))

    @pl.when(jnp.logical_not(has_far))
    def _():
        near[FAR] = jnp.zeros(near.shape[1:], BF16)
        for e in range(2 * ITERS + 1):
            halo[e, FAR] = jnp.zeros((rows, h), BF16)

    for it in range(ITERS):
        for edge in (0, n + 1):
            part_out[it, edge] = jnp.zeros(part_out.shape[2:], BF16)

    def trade(source, target, send, recv, side):
        return pltpu.make_async_remote_copy(
            src_ref=source, dst_ref=target, send_sem=send, recv_sem=recv,
            device_id={"sub": towards[side]}, device_id_type=MESH)

    def halo_copy(e, side):
        return trade(
            sent.at[e, :, part[side]], halo.at[e, side], halo_send.at[e, side], halo_recv.at[e, side], side)

    def near_copy(e, side):
        return trade(basis.at[pl.ds(0, nc), part[side]], near.at[side], near_send.at[side], near_recv.at[side], side)

    def only(side, act):
        if side == FAR:
            pl.when(has_far)(act)
        else:
            act()

    def begin(copy, e, side):
        only(side, lambda: copy(e, side).start())

    def arrive(copy, e, side):
        only(side, lambda: copy(e, side).wait_recv())

    def finish(copy, e, side):
        only(side, lambda: copy(e, side).wait_send())

    pieces = PIECES if relayed and maps.shape[1] % (16 * PIECES) == 0 else 1
    tall = maps.shape[1] // pieces

    def map_copy(peer, slot, piece, send):
        block = maps.at[slot, pl.ds(piece * tall, tall), :]
        return pltpu.make_async_remote_copy(
            src_ref=block, dst_ref=block, send_sem=send, recv_sem=map_recv.at[slot, piece],
            device_id={"col": peer}, device_id_type=MESH)

    def own_copy(peer, piece):
        return map_copy(peer, me_c, piece, map_send.at[peer, piece])

    def down_maps(act):
        for gap in range(reach, 0, -1):
            for piece in range(pieces):
                @pl.when(me_c >= gap)
                def _():
                    act(own_copy(me_c - gap, piece))

    def up_maps(act, wait):
        for gap in range(reach, 0, -1):
            @pl.when(me_c + gap < m)
            def _():
                if wait:
                    pl.semaphore_wait(entered.at[me_c + gap], 1)
                for piece in range(pieces):
                    act(own_copy(me_c + gap, piece))

    def relay_copy(peer, slot, piece):
        return map_copy(peer, slot, piece, relay_send.at[piece])

    def relay(first, last):
        if relayed:
            for piece in range(first, min(last, pieces)):
                @pl.when(me_c == 1)
                def _():
                    relay_copy(1, m - 1, piece).wait_recv()
                    relay_copy(0, m - 1, piece).start()

                @pl.when(me_c == m - 2)
                def _():
                    relay_copy(m - 2, 0, piece).wait_recv()
                    relay_copy(m - 1, 0, piece).start()

    def relay_done():
        if relayed:
            for piece in range(pieces):
                @pl.when(me_c == 1)
                def _():
                    relay_copy(0, m - 1, piece).wait_send()

                @pl.when(me_c == m - 2)
                def _():
                    relay_copy(m - 1, 0, piece).wait_send()

    upper = me_c < m // 2
    shift = ((me_c == 1) | (me_c == m - 2)).astype(jnp.int32) if relayed else 0
    turns = [lax.rem(i - shift + m, m) for i in range(m)]
    order = [jnp.where(upper, turn, m - 1 - turn) for turn in turns]
    early = -(-full * LANES // per)

    def maps_wait(first, last):
        for j in order[first:last]:
            known = (me_c == 1) & (j == m - 1) | (me_c == m - 2) & (j == 0) if relayed else me_c < 0

            @pl.when((j != me_c) & jnp.logical_not(known))
            def _():
                for piece in range(pieces):
                    relay_copy(me_c, j, piece).wait_recv()

    mains = rows * full

    def part_copy(it, peer, slot, kind):
        if kind < 2:
            lines = (pl.ds(0, mains), pl.ds(mains, rows // 2))[kind]
            source, target = part_out.at[it, pl.ds(peer, 3), lines], part_in.at[it, slot, :, lines]
        else:
            source, target = part_out.at[it, pl.ds(peer + lax.rem(peer, 2), 2)], part_in.at[it, slot, pl.ds(0, 2)]
        return pltpu.make_async_remote_copy(
            src_ref=source, dst_ref=target,
            send_sem=part_send.at[it, kind % 2, peer], recv_sem=part_recv.at[it, kind % 2, slot],
            device_id={"sub": peer}, device_id_type=MESH)

    def part_start(it, kind):
        for k in sorted(range(1, n), key=lambda k: -min(k, n - k)):
            part_copy(it, lax.rem(me_s + k, n), me_s, kind).start()

    def part_wait(it, kind):
        for k in range(1, n):
            part_copy(it, me_s, lax.rem(me_s + k, n), kind).wait_recv()

    get_state.wait()
    sent[0] = cur[...].astype(BF16)
    get_map.wait()
    mine = own[...]
    mine = jnp.concatenate([mine, mine[nc - TAIL :]], axis=0)
    maps[me_c] = fold(dot_nt(diagonal(n * per), mine), full).astype(BF16)

    pl.semaphore_wait(barrier, n - 1 + lax.min(me_c, reach))
    begin(halo_copy, 0, FAR)
    begin(halo_copy, 0, NEAR)
    down_maps(lambda copy: copy.start())
    for gap in range(1, reach + 1):
        @pl.when(me_c >= gap)
        def _():
            pl.semaphore_signal(entered.at[me_c], inc=1, device_id={"col": me_c - gap}, device_id_type=MESH)

    def stack(s, low, high):
        def gather(at):
            found = []
            for i in range(low // per, -(-high // per)):
                first, last = max(low - i * per, 0), min(high - i * per, per)
                found.append(maps[order[i], at + s * per + first : at + s * per + last, :])
            if per % 16:
                return jnp.concatenate([piece.astype(F32) for piece in found], axis=0).astype(BF16)
            return jnp.concatenate(found, axis=0)

        tail_at = full * n * per - (n // 2 * per if s >= n // 2 else 0)
        return jnp.concatenate([gather(f * n * per) for f in range(full)] + [gather(tail_at)], axis=1)

    def coefficients(rb):
        wide = dot_nt(rb, basis[...])
        lane = lanes_of(wide)
        low = jnp.where(lane < nc, wide, 0.0).astype(BF16)
        high = jnp.where((lane < full * LANES) | (lane >= nc), wide, 0.0).astype(BF16)
        return low, high

    def main_parts(it, sides):
        for s in range(n):
            wide = dot_nt(sides[s >= n // 2], stack(s, 0, full * LANES))
            wide = jnp.concatenate([wide[:, f * LANES : (f + 1) * LANES] for f in range(full)], axis=0)
            part_out[it, s + 1, pl.ds(0, mains)] = wide.astype(BF16)

    def tail_parts(it, sides):
        for s in range(n):
            block = stack(s, nc - TAIL, nc)
            tail = dot_nt(sides[s >= n // 2], jnp.concatenate([block, block], axis=0))
            part_out[it, s + 1, pl.ds(mains, rows // 2)] = fold_tail(tail).astype(BF16)

    def whole_parts(it, sides):
        for s in range(n):
            block = stack(s, 0, nc)
            wide = dot_nt(sides[s >= n // 2], jnp.concatenate([block, block[nc - TAIL :]], axis=0))
            part_out[it, s + 1] = fold(wide, full).astype(BF16)

    def coarse(it, count):
        total = part_in[it, 0, 0:count].astype(F32)
        for s in range(1, n):
            total = total + part_in[it, s, 0:count].astype(F32)
        return [unfold(total[i], rows, full).astype(BF16) for i in range(count)]

    def lift_operator():
        row = lax.broadcasted_iota(jnp.int32, (deep, nc), 0)
        row = jnp.where(row < nc, row, row - TAIL)
        source = row
        for i in range(m):
            here = (row >= i * per) & (row < (i + 1) * per)
            source = jnp.where(here, row + (order[i] - i) * per, source)
        place = (lax.broadcasted_iota(jnp.int32, (deep, nc), 1) == source).astype(F32).astype(BF16)

        def put(i, value):
            value = dot(place, value.astype(BF16)).astype(BF16)
            lifted[pl.ds(pl.multiple_of(i * deep, deep), deep), :] = value

        raised[...] = dot(place, basis[:nc]).astype(BF16)
        put(1, dot(basis[:nc], diag[...]))
        for side, i in ((NEAR, 2 * (1 - odd)), (FAR, 2 * odd)):
            arrive(near_copy, 0, side)
            put(i, dot(near[side], rim[part[side], :]))

    def permuted_inverse():
        used = ov[...]
        slot = lax.broadcasted_iota(jnp.int32, used.shape, 1)
        used = jnp.where(slot < count[...], used, -1)
        chunk = 2 * h // 4
        for i in range(4):
            place = lax.broadcasted_iota(jnp.int32, (chunk, slots), 0) + i * chunk
            pick = (place == used).astype(F32).astype(BF16)
            invp[i * chunk : (i + 1) * chunk, :] = dot(pick, inv[half:, :]).astype(BF16)
            if i > 0:
                relay(i - 1, i)

    def own_and_near(e, weights, margin):
        base[...] = dot(sent[e], weights)
        arrive(halo_copy, e, NEAR)
        base[...] += dot(halo[e, NEAR], margin[part[NEAR], :])

    def far_part(e, margin, columns):
        return dot(halo[e, FAR], margin[part[FAR], columns])

    def residual(e, columns, product):
        v = cur[:, columns]
        sent[e, :, columns] = (load[:, columns] - product - cubic_coef * v * v * v).astype(BF16)

    get_diag.wait()
    base[...] = dot(sent[0], diag[...])
    up_maps(lambda copy: copy.start(), True)
    get_basis.wait()
    get_again.wait()
    begin(near_copy, 0, FAR)
    begin(near_copy, 0, NEAR)
    get_rim.wait()
    arrive(halo_copy, 0, NEAR)
    base[...] += dot(halo[0, NEAR], rim[part[NEAR], :])
    get_load.wait()
    arrive(halo_copy, 0, FAR)
    for side in (FAR, NEAR):
        residual(1, part[side], base[:, part[side]] + far_part(0, rim, part[side]))
        begin(halo_copy, 1, side)

    for it in range(ITERS):
        first, last = it == 0, it == ITERS - 1
        e = 2 * it + 1
        if first:
            get_inv.wait()
            get_ov.wait()
            get_count.wait()
            permuted_inverse()
        else:
            whole_parts(it, coefficients(sent[e]))
            part_start(it, 2)
            part_in[it, me_s, 0:2] = part_out[it, pl.ds(me_s + odd, 2)]
        own_and_near(e, inv[:half, :], invp)
        arrive(halo_copy, e, FAR)
        for side in (FAR, NEAR):
            v = cur[:, part[side]] + (base[:, part[side]] + far_part(e, invp, part[side]))
            cur[:, part[side]] = v
            sent[e + 1, :, part[side]] = v.astype(BF16)
            if first or side == FAR:
                begin(halo_copy, e + 1, side)
        if first:
            relay(3, pieces)
            sides = coefficients(sent[e])
            maps_wait(0, early)
            main_parts(it, sides)
            part_start(it, 0)
            maps_wait(early, m)
            tail_parts(it, sides)
            part_start(it, 1)
            part_in[it, me_s] = part_out[it, pl.ds(me_s, 3)]
            own_and_near(e + 1, diag[...], rim)
            lift_operator()
            e = e + 1
            arrive(halo_copy, e, FAR)
            base[...] += far_part(e, rim, slice(None))
            part_wait(it, 0)
            part_wait(it, 1)
            three = coarse(it, 3)
            mine, three = three[1], jnp.concatenate(three, axis=1)
            for side in (FAR, NEAR):
                cur[:, part[side]] += dot(mine, raised[:, part[side]])
                residual(e + 1, part[side], base[:, part[side]] + dot(three, lifted[:, part[side]]))
                begin(halo_copy, e + 1, side)
        else:
            e = e + 1
            base[...] = dot(sent[e], diag[...])
            part_wait(it, 2)
            pair = coarse(it, 2)
            mine = jnp.where(odd == 1, pair[0].astype(F32), pair[1].astype(F32)).astype(BF16)
            change = dot(mine, raised[...])
            if last:
                before_ref[...] = cur[...]
                change_ref[...] = change
            cur[...] += change
            sent[e, :, part[NEAR]] = cur[:, part[NEAR]].astype(BF16)
            begin(halo_copy, e, NEAR)
            both = pl.ds(pl.multiple_of(odd * deep, deep), 2 * deep)
            base[...] += dot(jnp.concatenate(pair, axis=1), lifted[both, :])
            arrive(halo_copy, e, NEAR)
            base[...] += dot(halo[e, NEAR], rim[part[NEAR], :])
            arrive(halo_copy, e, FAR)
            for side in (FAR, NEAR):
                product = base[:, part[side]] + far_part(e, rim, part[side])
                if last:
                    applied_ref[:, part[side]] = product
                else:
                    residual(e + 1, part[side], product)
                    begin(halo_copy, e + 1, side)

    for side in (FAR, NEAR):
        for e in range(2 * ITERS + 1):
            finish(halo_copy, e, side)
        finish(near_copy, 0, side)
    down_maps(lambda copy: copy.wait_send())
    up_maps(lambda copy: copy.wait_send(), False)
    relay_done()
    for it in range(ITERS):
        for kind in (0, 1) if it == 0 else (2,):
            for k in range(1, n):
                part_copy(it, lax.rem(me_s + k, n), me_s, kind).wait_send()


def body(n, m, state_init, load_cols, stiff_diag, stiff_rim, inverse, ov_rows, ov_count, coarse_basis, coarse_map):
    rows, width = state_init.shape
    h = stiff_rim.shape[0] // 2
    basis_t = coarse_basis.T
    nc = basis_t.shape[0]
    if nc % LANES != TAIL or n % 2 or rows % 32 or width != 2 * h:
        raise ValueError("unsupported sizes")
    full = nc // LANES
    trades = 2 * ITERS + 1
    packed = (rows * full + rows // 2, LANES)
    hbm = pl.BlockSpec(memory_space=pltpu.HBM)
    vmem = pl.BlockSpec(memory_space=pltpu.VMEM)
    dma = pltpu.SemaphoreType.DMA
    out = jax.ShapeDtypeStruct((rows, width), F32)
    before, change, product = pl.pallas_call(
        functools.partial(kernel, n, m),
        out_shape=(out, out, out),
        in_specs=[hbm] * 9,
        out_specs=(vmem, vmem, vmem),
        scratch_shapes=[
            pltpu.VMEM((rows, width), F32),
            pltpu.VMEM((rows, width), F32),
            pltpu.VMEM((rows, width), F32),
            pltpu.VMEM(stiff_diag.shape, BF16),
            pltpu.VMEM(stiff_rim.shape, BF16),
            pltpu.VMEM(inverse.shape, BF16),
            pltpu.VMEM(ov_rows.shape, jnp.int32),
            pltpu.VMEM((1, 1), jnp.int32),
            pltpu.VMEM((nc + TAIL, width), BF16),
            pltpu.VMEM((nc + TAIL, width), BF16),
            pltpu.VMEM((2, nc, h), BF16),
            pltpu.VMEM((3 * (nc + TAIL), width), BF16),
            pltpu.VMEM(coarse_map.shape, BF16),
            pltpu.VMEM((m, coarse_map.shape[1] * full + coarse_map.shape[1] // 2, LANES), BF16),
            pltpu.VMEM((2 * h, width), BF16),
            pltpu.VMEM((trades, rows, width), BF16),
            pltpu.VMEM((trades, 2, rows, h), BF16),
            pltpu.VMEM((ITERS, n + 2) + packed, BF16),
            pltpu.VMEM((ITERS, n, 3) + packed, BF16),
            dma((10,)),
            dma((trades, 2)),
            dma((trades, 2)),
            dma((2,)),
            dma((2,)),
            dma((m, PIECES)),
            dma((m, PIECES)),
            dma((PIECES,)),
            dma((ITERS, 2, n)),
            dma((ITERS, 2, n)),
            pltpu.SemaphoreType.REGULAR((m,)),
        ],
        compiler_params=pltpu.CompilerParams(collective_id=0, has_side_effects=True, vmem_limit_bytes=60 * 2**20),
        name="schwarz",
    )(state_init, load_cols, stiff_diag, stiff_rim, inverse, ov_rows, ov_count.reshape(1, 1), basis_t, coarse_map)
    current = before + change
    return current, load_cols - product - cubic_coef * current * current * current


def solution(mesh):
    in_specs = (
        P("col", "sub"),
        P("col", "sub"),
        P(None, "sub"),
        P(None, "sub"),
        P(None, "sub"),
        P("sub", None),
        P("sub"),
        P("sub", None),
        P("sub", "col"),
    )
    out_specs = (P("col", "sub"), P("col", "sub"))
    step = functools.partial(body, mesh.shape["sub"], mesh.shape["col"])
    return jax.shard_map(step, mesh=mesh, in_specs=in_specs, out_specs=out_specs, check_vma=False)
```

```python
import functools

import jax
import jax.numpy as jnp
from jax import lax
from jax.experimental import pallas as pl
from jax.experimental.pallas import tpu as pltpu
from jax.sharding import PartitionSpec as P

ITERS = 2
PIECES = 4

cubic_coef = 0.1
MESH = pl.DeviceIdType.MESH
F32 = jnp.float32
BF16 = jnp.bfloat16


NEAR, FAR = 0, 1
TAIL = 64
LANES = 128


def dot(a, b):
    return jnp.dot(a, b, preferred_element_type=F32)


def dot_nt(a, b):
    return lax.dot_general(a, b, (((1,), (1,)), ((), ())), preferred_element_type=F32)


def diagonal(size):
    place = [lax.broadcasted_iota(jnp.int32, (size, size), axis) for axis in (0, 1)]
    return (place[0] == place[1]).astype(F32).astype(BF16)


def lanes_of(value):
    return lax.broadcasted_iota(jnp.int32, value.shape, 1)


def fold_tail(tail):
    half = tail.shape[0] // 2
    return jnp.where(lanes_of(tail[:half]) < TAIL, tail[:half], tail[half:])


def fold(wide, full):
    blocks = [wide[:, f * LANES : (f + 1) * LANES] for f in range(full)]
    return jnp.concatenate(blocks + [fold_tail(wide[:, full * LANES :])], axis=0)


def unfold(packed, rows, full):
    tail = packed[rows * full :]
    tail = jnp.concatenate([tail, tail], axis=0)
    upper = lax.broadcasted_iota(jnp.int32, tail.shape, 0) < rows // 2
    tail = jnp.where(upper == (lanes_of(tail) < TAIL), tail, jnp.zeros_like(tail))
    return jnp.concatenate([packed[f * rows : (f + 1) * rows] for f in range(full)] + [tail], axis=1)


def kernel(
    n, m,
    state_hbm, load_hbm, diag_hbm, rim_hbm, inv_hbm, ov_hbm, count_hbm, basis_hbm, map_hbm,
    before_ref, change_ref, applied_ref,
    cur, load, base, diag, rim, inv, ov, count, basis, raised, near, lifted, own, maps, invp,
    sent, halo, part_out, part_in,
    local_sem, halo_send, halo_recv, near_send, near_recv, map_send, map_recv, relay_send, part_send, part_recv, entered,
):
    me_s = lax.axis_index("sub")
    me_c = lax.axis_index("col")
    rows, width = cur.shape
    h = halo.shape[3]
    nc = near.shape[1]
    per = nc // m
    full = nc // LANES
    slots = ov.shape[1]
    half = inv.shape[0] - slots
    deep = nc + TAIL
    relayed = m >= 4
    reach = m - 1 - relayed

    barrier = pltpu.get_barrier_semaphore()
    for k in range(1, n):
        pl.semaphore_signal(barrier, inc=1, device_id={"sub": lax.rem(me_s + k, n)}, device_id_type=MESH)
    for gap in range(1, reach + 1):
        @pl.when(me_c + gap < m)
        def _():
            pl.semaphore_signal(barrier, inc=1, device_id={"col": me_c + gap}, device_id_type=MESH)

    def fetch(index, source, target):
        copy = pltpu.make_async_copy(source, target, local_sem.at[index])
        copy.start()
        return copy

    get_state = fetch(0, state_hbm, cur)
    get_map = fetch(1, map_hbm, own)
    get_diag = fetch(2, diag_hbm, diag)
    get_basis = fetch(3, basis_hbm, basis.at[pl.ds(0, nc)])
    get_again = fetch(4, basis_hbm.at[pl.ds(nc - TAIL, TAIL)], basis.at[pl.ds(nc, TAIL)])
    get_rim = fetch(5, rim_hbm, rim)
    get_load = fetch(6, load_hbm, load)
    get_ov = fetch(7, ov_hbm, ov)
    get_count = fetch(8, count_hbm, count)
    get_inv = fetch(9, inv_hbm, inv)

    odd = lax.rem(me_s, 2)
    has_far = (me_s > 0) & (me_s < n - 1)
    towards = (lax.rem(me_s + n + 1 - 2 * odd, n), lax.rem(me_s + n - 1 + 2 * odd, n))
    part = tuple(pl.ds(pl.multiple_of(at, h), h) for at in ((1 - odd) * h, odd * h))

    @pl.when(jnp.logical_not(has_far))
    def _():
        near[FAR] = jnp.zeros(near.shape[1:], BF16)
        for e in range(2 * ITERS + 1):
            halo[e, FAR] = jnp.zeros((rows, h), BF16)

    for it in range(ITERS):
        for edge in (0, n + 1):
            part_out[it, edge] = jnp.zeros(part_out.shape[2:], BF16)

    def trade(source, target, send, recv, side):
        return pltpu.make_async_remote_copy(
            src_ref=source, dst_ref=target, send_sem=send, recv_sem=recv,
            device_id={"sub": towards[side]}, device_id_type=MESH)

    def halo_copy(e, side):
        return trade(
            sent.at[e, :, part[side]], halo.at[e, side], halo_send.at[e, side], halo_recv.at[e, side], side)

    def near_copy(e, side):
        return trade(basis.at[pl.ds(0, nc), part[side]], near.at[side], near_send.at[side], near_recv.at[side], side)

    def only(side, act):
        if side == FAR:
            pl.when(has_far)(act)
        else:
            act()

    def begin(copy, e, side):
        only(side, lambda: copy(e, side).start())

    def arrive(copy, e, side):
        only(side, lambda: copy(e, side).wait_recv())

    def finish(copy, e, side):
        only(side, lambda: copy(e, side).wait_send())

    pieces = PIECES if relayed and maps.shape[1] % (16 * PIECES) == 0 else 1
    tall = maps.shape[1] // pieces

    def map_copy(peer, slot, piece, send):
        block = maps.at[slot, pl.ds(piece * tall, tall), :]
        return pltpu.make_async_remote_copy(
            src_ref=block, dst_ref=block, send_sem=send, recv_sem=map_recv.at[slot, piece],
            device_id={"col": peer}, device_id_type=MESH)

    def own_copy(peer, piece):
        return map_copy(peer, me_c, piece, map_send.at[peer, piece])

    def down_maps(act):
        for gap in range(reach, 0, -1):
            for piece in range(pieces):
                @pl.when(me_c >= gap)
                def _():
                    act(own_copy(me_c - gap, piece))

    def up_maps(act, wait):
        for gap in range(reach, 0, -1):
            @pl.when(me_c + gap < m)
            def _():
                if wait:
                    pl.semaphore_wait(entered.at[me_c + gap], 1)
                for piece in range(pieces):
                    act(own_copy(me_c + gap, piece))

    def relay_copy(peer, slot, piece):
        return map_copy(peer, slot, piece, relay_send.at[piece])

    def relay(first, last):
        if relayed:
            for piece in range(first, min(last, pieces)):
                @pl.when(me_c == 1)
                def _():
                    relay_copy(1, m - 1, piece).wait_recv()
                    relay_copy(0, m - 1, piece).start()

                @pl.when(me_c == m - 2)
                def _():
                    relay_copy(m - 2, 0, piece).wait_recv()
                    relay_copy(m - 1, 0, piece).start()

    def relay_done():
        if relayed:
            for piece in range(pieces):
                @pl.when(me_c == 1)
                def _():
                    relay_copy(0, m - 1, piece).wait_send()

                @pl.when(me_c == m - 2)
                def _():
                    relay_copy(m - 1, 0, piece).wait_send()

    upper = me_c < m // 2
    shift = ((me_c == 1) | (me_c == m - 2)).astype(jnp.int32) if relayed else 0
    turns = [lax.rem(i - shift + m, m) for i in range(m)]
    order = [jnp.where(upper, turn, m - 1 - turn) for turn in turns]
    early = -(-full * LANES // per)

    def maps_wait(first, last):
        for j in order[first:last]:
            known = (me_c == 1) & (j == m - 1) | (me_c == m - 2) & (j == 0) if relayed else me_c < 0

            @pl.when((j != me_c) & jnp.logical_not(known))
            def _():
                for piece in range(pieces):
                    relay_copy(me_c, j, piece).wait_recv()

    mains = rows * full

    def part_copy(it, peer, slot, kind):
        if kind < 2:
            lines = (pl.ds(0, mains), pl.ds(mains, rows // 2))[kind]
            source, target = part_out.at[it, pl.ds(peer, 3), lines], part_in.at[it, slot, :, lines]
        else:
            source, target = part_out.at[it, pl.ds(peer + lax.rem(peer, 2), 2)], part_in.at[it, slot, pl.ds(0, 2)]
        return pltpu.make_async_remote_copy(
            src_ref=source, dst_ref=target,
            send_sem=part_send.at[it, kind % 2, peer], recv_sem=part_recv.at[it, kind % 2, slot],
            device_id={"sub": peer}, device_id_type=MESH)

    def part_start(it, kind):
        for k in range(1, n):
            part_copy(it, lax.rem(me_s + k, n), me_s, kind).start()

    def part_wait(it, kind):
        for k in range(1, n):
            part_copy(it, me_s, lax.rem(me_s + k, n), kind).wait_recv()

    get_state.wait()
    sent[0] = cur[...].astype(BF16)
    get_map.wait()
    mine = own[...]
    mine = jnp.concatenate([mine, mine[nc - TAIL :]], axis=0)
    maps[me_c] = fold(dot_nt(diagonal(n * per), mine), full).astype(BF16)

    pl.semaphore_wait(barrier, n - 1 + lax.min(me_c, reach))
    begin(halo_copy, 0, FAR)
    begin(halo_copy, 0, NEAR)
    down_maps(lambda copy: copy.start())
    for gap in range(1, reach + 1):
        @pl.when(me_c >= gap)
        def _():
            pl.semaphore_signal(entered.at[me_c], inc=1, device_id={"col": me_c - gap}, device_id_type=MESH)

    def stack(s, low, high):
        def gather(at):
            found = []
            for i in range(low // per, -(-high // per)):
                first, last = max(low - i * per, 0), min(high - i * per, per)
                found.append(maps[order[i], at + s * per + first : at + s * per + last, :])
            if per % 16:
                return jnp.concatenate([piece.astype(F32) for piece in found], axis=0).astype(BF16)
            return jnp.concatenate(found, axis=0)

        tail_at = full * n * per - (n // 2 * per if s >= n // 2 else 0)
        return jnp.concatenate([gather(f * n * per) for f in range(full)] + [gather(tail_at)], axis=1)

    def coefficients(rb):
        wide = dot_nt(rb, basis[...])
        lane = lanes_of(wide)
        low = jnp.where(lane < nc, wide, 0.0).astype(BF16)
        high = jnp.where((lane < full * LANES) | (lane >= nc), wide, 0.0).astype(BF16)
        return low, high

    def main_parts(it, sides):
        for s in range(n):
            wide = dot_nt(sides[s >= n // 2], stack(s, 0, full * LANES))
            wide = jnp.concatenate([wide[:, f * LANES : (f + 1) * LANES] for f in range(full)], axis=0)
            part_out[it, s + 1, pl.ds(0, mains)] = wide.astype(BF16)

    def tail_parts(it, sides):
        for s in range(n):
            block = stack(s, nc - TAIL, nc)
            tail = dot_nt(sides[s >= n // 2], jnp.concatenate([block, block], axis=0))
            part_out[it, s + 1, pl.ds(mains, rows // 2)] = fold_tail(tail).astype(BF16)

    def whole_parts(it, sides):
        for s in range(n):
            block = stack(s, 0, nc)
            wide = dot_nt(sides[s >= n // 2], jnp.concatenate([block, block[nc - TAIL :]], axis=0))
            part_out[it, s + 1] = fold(wide, full).astype(BF16)
            for peer in (s - 1, s) if s % 2 == 0 else (s,) if s == n - 1 else ():
                if peer >= 0:
                    @pl.when(me_s != peer)
                    def _():
                        part_copy(it, peer, me_s, 2).start()

    def gathered(it, lines):
        total = part_in[it, 0, :, lines].astype(F32)
        for s in range(1, n):
            total = total + part_in[it, s, :, lines].astype(F32)
        return total

    def coarse(it, count):
        total = part_in[it, 0, 0:count].astype(F32)
        for s in range(1, n):
            total = total + part_in[it, s, 0:count].astype(F32)
        return [unfold(total[i], rows, full).astype(BF16) for i in range(count)]

    def lift_operator():
        row = lax.broadcasted_iota(jnp.int32, (deep, nc), 0)
        row = jnp.where(row < nc, row, row - TAIL)
        source = row
        for i in range(m):
            here = (row >= i * per) & (row < (i + 1) * per)
            source = jnp.where(here, row + (order[i] - i) * per, source)
        place = (lax.broadcasted_iota(jnp.int32, (deep, nc), 1) == source).astype(F32).astype(BF16)

        def put(i, value):
            value = dot(place, value.astype(BF16)).astype(BF16)
            lifted[pl.ds(pl.multiple_of(i * deep, deep), deep), :] = value

        raised[...] = dot(place, basis[:nc]).astype(BF16)
        put(1, dot(basis[:nc], diag[...]))
        for side, i in ((NEAR, 2 * (1 - odd)), (FAR, 2 * odd)):
            arrive(near_copy, 0, side)
            put(i, dot(near[side], rim[part[side], :]))

    def permuted_inverse():
        used = ov[...]
        slot = lax.broadcasted_iota(jnp.int32, used.shape, 1)
        used = jnp.where(slot < count[...], used, -1)
        chunk = 2 * h // 4
        for i in range(4):
            place = lax.broadcasted_iota(jnp.int32, (chunk, slots), 0) + i * chunk
            pick = (place == used).astype(F32).astype(BF16)
            invp[i * chunk : (i + 1) * chunk, :] = dot(pick, inv[half:, :]).astype(BF16)
            if i > 0:
                relay(i - 1, i)

    def own_and_near(e, weights, margin):
        base[...] = dot(sent[e], weights)
        arrive(halo_copy, e, NEAR)
        base[...] += dot(halo[e, NEAR], margin[part[NEAR], :])

    def far_part(e, margin, columns):
        return dot(halo[e, FAR], margin[part[FAR], columns])

    def residual(e, columns, product):
        v = cur[:, columns]
        sent[e, :, columns] = (load[:, columns] - product - cubic_coef * v * v * v).astype(BF16)

    get_diag.wait()
    base[...] = dot(sent[0], diag[...])
    up_maps(lambda copy: copy.start(), True)
    get_basis.wait()
    get_again.wait()
    begin(near_copy, 0, FAR)
    begin(near_copy, 0, NEAR)
    get_rim.wait()
    arrive(halo_copy, 0, NEAR)
    base[...] += dot(halo[0, NEAR], rim[part[NEAR], :])
    get_load.wait()
    arrive(halo_copy, 0, FAR)
    for side in (FAR, NEAR):
        residual(1, part[side], base[:, part[side]] + far_part(0, rim, part[side]))
        begin(halo_copy, 1, side)

    for it in range(ITERS):
        first, last = it == 0, it == ITERS - 1
        e = 2 * it + 1
        if first:
            get_inv.wait()
            get_ov.wait()
            get_count.wait()
            permuted_inverse()
        else:
            whole_parts(it, coefficients(sent[e]))
            part_in[it, me_s, 0:2] = part_out[it, pl.ds(me_s + odd, 2)]
        own_and_near(e, inv[:half, :], invp)
        if first:
            relay(3, pieces)
        arrive(halo_copy, e, FAR)
        for side in (FAR, NEAR):
            v = cur[:, part[side]] + (base[:, part[side]] + far_part(e, invp, part[side]))
            cur[:, part[side]] = v
            sent[e + 1, :, part[side]] = v.astype(BF16)
            if first or side == FAR:
                begin(halo_copy, e + 1, side)
        if first:
            sides = coefficients(sent[e])
            maps_wait(0, early)
            main_parts(it, sides)
            part_start(it, 0)
            maps_wait(early, m)
            tail_parts(it, sides)
            part_start(it, 1)
            part_in[it, me_s] = part_out[it, pl.ds(me_s, 3)]
            own_and_near(e + 1, diag[...], rim)
            lift_operator()
            e = e + 1
            arrive(halo_copy, e, FAR)
            base[...] += far_part(e, rim, slice(None))
            part_wait(it, 0)
            total = [gathered(it, pl.ds(0, mains))]
            part_wait(it, 1)
            total = jnp.concatenate(total + [gathered(it, pl.ds(mains, rows // 2))], axis=1)
            three = [unfold(total[i], rows, full).astype(BF16) for i in range(3)]
            mine, three = three[1], jnp.concatenate(three, axis=1)
            for side in (FAR, NEAR):
                cur[:, part[side]] += dot(mine, raised[:, part[side]])
                residual(e + 1, part[side], base[:, part[side]] + dot(three, lifted[:, part[side]]))
                begin(halo_copy, e + 1, side)
        else:
            e = e + 1
            base[...] = dot(sent[e], diag[...])
            part_wait(it, 2)
            pair = coarse(it, 2)
            mine = jnp.where(odd == 1, pair[0].astype(F32), pair[1].astype(F32)).astype(BF16)
            for side in (NEAR, FAR):
                columns = part[side]
                change = dot(mine, raised[:, columns])
                v = cur[:, columns]
                if last:
                    before_ref[:, columns] = v
                    change_ref[:, columns] = change
                else:
                    cur[:, columns] = v + change
                if side == NEAR:
                    sent[e, :, columns] = (v + change).astype(BF16)
                    begin(halo_copy, e, NEAR)
            both = pl.ds(pl.multiple_of(odd * deep, deep), 2 * deep)
            base[...] += dot(jnp.concatenate(pair, axis=1), lifted[both, :])
            arrive(halo_copy, e, NEAR)
            base[...] += dot(halo[e, NEAR], rim[part[NEAR], :])
            arrive(halo_copy, e, FAR)
            for side in (FAR, NEAR):
                product = base[:, part[side]] + far_part(e, rim, part[side])
                if last:
                    applied_ref[:, part[side]] = product
                else:
                    residual(e + 1, part[side], product)
                    begin(halo_copy, e + 1, side)

    for side in (FAR, NEAR):
        for e in range(2 * ITERS + 1):
            finish(halo_copy, e, side)
        finish(near_copy, 0, side)
    down_maps(lambda copy: copy.wait_send())
    up_maps(lambda copy: copy.wait_send(), False)
    relay_done()
    for it in range(ITERS):
        for kind in (0, 1) if it == 0 else (2,):
            for k in range(1, n):
                part_copy(it, lax.rem(me_s + k, n), me_s, kind).wait_send()


def body(n, m, state_init, load_cols, stiff_diag, stiff_rim, inverse, ov_rows, ov_count, coarse_basis, coarse_map):
    rows, width = state_init.shape
    h = stiff_rim.shape[0] // 2
    basis_t = coarse_basis.T
    nc = basis_t.shape[0]
    if nc % LANES != TAIL or n % 2 or rows % 32 or width != 2 * h:
        raise ValueError("unsupported sizes")
    full = nc // LANES
    trades = 2 * ITERS + 1
    packed = (rows * full + rows // 2, LANES)
    hbm = pl.BlockSpec(memory_space=pltpu.HBM)
    vmem = pl.BlockSpec(memory_space=pltpu.VMEM)
    dma = pltpu.SemaphoreType.DMA
    out = jax.ShapeDtypeStruct((rows, width), F32)
    before, change, product = pl.pallas_call(
        functools.partial(kernel, n, m),
        out_shape=(out, out, out),
        in_specs=[hbm] * 9,
        out_specs=(vmem, vmem, vmem),
        scratch_shapes=[
            pltpu.VMEM((rows, width), F32),
            pltpu.VMEM((rows, width), F32),
            pltpu.VMEM((rows, width), F32),
            pltpu.VMEM(stiff_diag.shape, BF16),
            pltpu.VMEM(stiff_rim.shape, BF16),
            pltpu.VMEM(inverse.shape, BF16),
            pltpu.VMEM(ov_rows.shape, jnp.int32),
            pltpu.VMEM((1, 1), jnp.int32),
            pltpu.VMEM((nc + TAIL, width), BF16),
            pltpu.VMEM((nc + TAIL, width), BF16),
            pltpu.VMEM((2, nc, h), BF16),
            pltpu.VMEM((3 * (nc + TAIL), width), BF16),
            pltpu.VMEM(coarse_map.shape, BF16),
            pltpu.VMEM((m, coarse_map.shape[1] * full + coarse_map.shape[1] // 2, LANES), BF16),
            pltpu.VMEM((2 * h, width), BF16),
            pltpu.VMEM((trades, rows, width), BF16),
            pltpu.VMEM((trades, 2, rows, h), BF16),
            pltpu.VMEM((ITERS, n + 2) + packed, BF16),
            pltpu.VMEM((ITERS, n, 3) + packed, BF16),
            dma((10,)),
            dma((trades, 2)),
            dma((trades, 2)),
            dma((2,)),
            dma((2,)),
            dma((m, PIECES)),
            dma((m, PIECES)),
            dma((PIECES,)),
            dma((ITERS, 2, n)),
            dma((ITERS, 2, n)),
            pltpu.SemaphoreType.REGULAR((m,)),
        ],
        compiler_params=pltpu.CompilerParams(collective_id=0, has_side_effects=True, vmem_limit_bytes=60 * 2**20),
        name="schwarz",
    )(state_init, load_cols, stiff_diag, stiff_rim, inverse, ov_rows, ov_count.reshape(1, 1), basis_t, coarse_map)
    current = before + change
    return current, load_cols - product - cubic_coef * current * current * current


def solution(mesh):
    in_specs = (
        P("col", "sub"),
        P("col", "sub"),
        P(None, "sub"),
        P(None, "sub"),
        P(None, "sub"),
        P("sub", None),
        P("sub"),
        P("sub", None),
        P("sub", "col"),
    )
    out_specs = (P("col", "sub"), P("col", "sub"))
    step = functools.partial(body, mesh.shape["sub"], mesh.shape["col"])
    return jax.shard_map(step, mesh=mesh, in_specs=in_specs, out_specs=out_specs, check_vma=False)
```

```python
import functools

import jax
import jax.numpy as jnp
from jax import lax
from jax.experimental import pallas as pl
from jax.experimental.pallas import tpu as pltpu
from jax.sharding import PartitionSpec as P

ITERS = 2
PIECES = 3

cubic_coef = 0.1
MESH = pl.DeviceIdType.MESH
F32 = jnp.float32
BF16 = jnp.bfloat16


NEAR, FAR = 0, 1
TAIL = 64
LANES = 128


def dot(a, b):
    return jnp.dot(a, b, preferred_element_type=F32)


def dot_nt(a, b):
    return lax.dot_general(a, b, (((1,), (1,)), ((), ())), preferred_element_type=F32)


def diagonal(size):
    place = [lax.broadcasted_iota(jnp.int32, (size, size), axis) for axis in (0, 1)]
    return (place[0] == place[1]).astype(F32).astype(BF16)


def lanes_of(value):
    return lax.broadcasted_iota(jnp.int32, value.shape, 1)


def fold_tail(tail):
    half = tail.shape[0] // 2
    return jnp.where(lanes_of(tail[:half]) < TAIL, tail[:half], tail[half:])


def fold(wide, full):
    blocks = [wide[:, f * LANES : (f + 1) * LANES] for f in range(full)]
    return jnp.concatenate(blocks + [fold_tail(wide[:, full * LANES :])], axis=0)


def unfold(packed, rows, full):
    tail = packed[rows * full :]
    tail = jnp.concatenate([tail, tail], axis=0)
    upper = lax.broadcasted_iota(jnp.int32, tail.shape, 0) < rows // 2
    tail = jnp.where(upper == (lanes_of(tail) < TAIL), tail, jnp.zeros_like(tail))
    return jnp.concatenate([packed[f * rows : (f + 1) * rows] for f in range(full)] + [tail], axis=1)


def kernel(
    n, m,
    state_hbm, load_hbm, diag_hbm, rim_hbm, inv_hbm, ov_hbm, count_hbm, basis_hbm, map_hbm,
    before_ref, change_ref, applied_ref,
    cur, load, base, diag, rim, inv, ov, count, basis, raised, near, lifted, own, maps, invp,
    sent, halo, part_out, part_in,
    local_sem, halo_send, halo_recv, near_send, near_recv, map_send, map_recv, relay_send, part_send, part_recv, entered,
):
    me_s = lax.axis_index("sub")
    me_c = lax.axis_index("col")
    rows, width = cur.shape
    h = halo.shape[3]
    nc = near.shape[1]
    per = nc // m
    full = nc // LANES
    slots = ov.shape[1]
    half = inv.shape[0] - slots
    deep = nc + TAIL
    relayed = m >= 4
    reach = m - 1 - relayed

    barrier = pltpu.get_barrier_semaphore()
    for k in range(1, n):
        pl.semaphore_signal(barrier, inc=1, device_id={"sub": lax.rem(me_s + k, n)}, device_id_type=MESH)
    for gap in range(1, reach + 1):
        @pl.when(me_c + gap < m)
        def _():
            pl.semaphore_signal(barrier, inc=1, device_id={"col": me_c + gap}, device_id_type=MESH)

    def fetch(index, source, target):
        copy = pltpu.make_async_copy(source, target, local_sem.at[index])
        copy.start()
        return copy

    get_state = fetch(0, state_hbm, cur)
    get_map = fetch(1, map_hbm, own)
    get_diag = fetch(2, diag_hbm, diag)
    get_basis = fetch(3, basis_hbm, basis.at[pl.ds(0, nc)])
    get_again = fetch(4, basis_hbm.at[pl.ds(nc - TAIL, TAIL)], basis.at[pl.ds(nc, TAIL)])
    get_rim = fetch(5, rim_hbm, rim)
    get_load = fetch(6, load_hbm, load)
    get_ov = fetch(7, ov_hbm, ov)
    get_count = fetch(8, count_hbm, count)
    get_inv = fetch(9, inv_hbm, inv)

    odd = lax.rem(me_s, 2)
    has_far = (me_s > 0) & (me_s < n - 1)
    towards = (lax.rem(me_s + n + 1 - 2 * odd, n), lax.rem(me_s + n - 1 + 2 * odd, n))
    part = tuple(pl.ds(pl.multiple_of(at, h), h) for at in ((1 - odd) * h, odd * h))

    @pl.when(jnp.logical_not(has_far))
    def _():
        near[FAR] = jnp.zeros(near.shape[1:], BF16)
        for e in range(2 * ITERS + 1):
            halo[e, FAR] = jnp.zeros((rows, h), BF16)

    for it in range(ITERS):
        for edge in (0, n + 1):
            part_out[it, edge] = jnp.zeros(part_out.shape[2:], BF16)

    def trade(source, target, send, recv, side):
        return pltpu.make_async_remote_copy(
            src_ref=source, dst_ref=target, send_sem=send, recv_sem=recv,
            device_id={"sub": towards[side]}, device_id_type=MESH)

    def halo_copy(e, side):
        return trade(
            sent.at[e, :, part[side]], halo.at[e, side], halo_send.at[e, side], halo_recv.at[e, side], side)

    def near_copy(e, side):
        return trade(basis.at[pl.ds(0, nc), part[side]], near.at[side], near_send.at[side], near_recv.at[side], side)

    def only(side, act):
        if side == FAR:
            pl.when(has_far)(act)
        else:
            act()

    def begin(copy, e, side):
        only(side, lambda: copy(e, side).start())

    def arrive(copy, e, side):
        only(side, lambda: copy(e, side).wait_recv())

    def finish(copy, e, side):
        only(side, lambda: copy(e, side).wait_send())

    pieces = PIECES if relayed and maps.shape[1] % (16 * PIECES) == 0 else 1
    tall = maps.shape[1] // pieces

    def map_copy(peer, slot, piece, send):
        block = maps.at[slot, pl.ds(piece * tall, tall), :]
        return pltpu.make_async_remote_copy(
            src_ref=block, dst_ref=block, send_sem=send, recv_sem=map_recv.at[slot, piece],
            device_id={"col": peer}, device_id_type=MESH)

    def own_copy(peer, piece):
        return map_copy(peer, me_c, piece, map_send.at[peer, piece])

    def down_maps(act):
        for gap in range(reach, 0, -1):
            for piece in range(pieces):
                @pl.when(me_c >= gap)
                def _():
                    act(own_copy(me_c - gap, piece))

    def up_maps(act, wait):
        for gap in range(reach, 0, -1):
            @pl.when(me_c + gap < m)
            def _():
                if wait:
                    pl.semaphore_wait(entered.at[me_c + gap], 1)
                for piece in range(pieces):
                    act(own_copy(me_c + gap, piece))

    def relay_copy(peer, slot, piece):
        return map_copy(peer, slot, piece, relay_send.at[piece])

    def relay(first, last):
        if relayed:
            for piece in range(first, min(last, pieces)):
                @pl.when(me_c == 1)
                def _():
                    relay_copy(1, m - 1, piece).wait_recv()
                    relay_copy(0, m - 1, piece).start()

                @pl.when(me_c == m - 2)
                def _():
                    relay_copy(m - 2, 0, piece).wait_recv()
                    relay_copy(m - 1, 0, piece).start()

    def relay_done():
        if relayed:
            for piece in range(pieces):
                @pl.when(me_c == 1)
                def _():
                    relay_copy(0, m - 1, piece).wait_send()

                @pl.when(me_c == m - 2)
                def _():
                    relay_copy(m - 1, 0, piece).wait_send()

    upper = me_c < m // 2
    shift = ((me_c == 1) | (me_c == m - 2)).astype(jnp.int32) if relayed else 0
    turns = [lax.rem(i - shift + m, m) for i in range(m)]
    order = [jnp.where(upper, turn, m - 1 - turn) for turn in turns]
    early = -(-full * LANES // per)

    def maps_wait(first, last):
        for j in order[first:last]:
            known = (me_c == 1) & (j == m - 1) | (me_c == m - 2) & (j == 0) if relayed else me_c < 0

            @pl.when((j != me_c) & jnp.logical_not(known))
            def _():
                for piece in range(pieces):
                    relay_copy(me_c, j, piece).wait_recv()

    mains = rows * full

    def part_copy(it, peer, slot, kind):
        if kind < 2:
            lines = (pl.ds(0, mains), pl.ds(mains, rows // 2))[kind]
            source, target = part_out.at[it, pl.ds(peer, 3), lines], part_in.at[it, slot, :, lines]
        else:
            source, target = part_out.at[it, pl.ds(peer + lax.rem(peer, 2), 2)], part_in.at[it, slot, pl.ds(0, 2)]
        return pltpu.make_async_remote_copy(
            src_ref=source, dst_ref=target,
            send_sem=part_send.at[it, kind % 2, peer], recv_sem=part_recv.at[it, kind % 2, slot],
            device_id={"sub": peer}, device_id_type=MESH)

    def part_start(it, kind):
        for k in range(1, n):
            part_copy(it, lax.rem(me_s + k, n), me_s, kind).start()

    def part_wait(it, kind):
        for k in range(1, n):
            part_copy(it, me_s, lax.rem(me_s + k, n), kind).wait_recv()

    get_state.wait()
    sent[0] = cur[...].astype(BF16)
    get_map.wait()
    mine = own[...]
    mine = jnp.concatenate([mine, mine[nc - TAIL :]], axis=0)
    maps[me_c] = fold(dot_nt(diagonal(n * per), mine), full).astype(BF16)

    pl.semaphore_wait(barrier, n - 1 + lax.min(me_c, reach))
    begin(halo_copy, 0, FAR)
    begin(halo_copy, 0, NEAR)
    down_maps(lambda copy: copy.start())
    for gap in range(1, reach + 1):
        @pl.when(me_c >= gap)
        def _():
            pl.semaphore_signal(entered.at[me_c], inc=1, device_id={"col": me_c - gap}, device_id_type=MESH)

    def stack(s, low, high):
        def gather(at):
            found = []
            for i in range(low // per, -(-high // per)):
                first, last = max(low - i * per, 0), min(high - i * per, per)
                found.append(maps[order[i], at + s * per + first : at + s * per + last, :])
            if per % 16:
                return jnp.concatenate([piece.astype(F32) for piece in found], axis=0).astype(BF16)
            return jnp.concatenate(found, axis=0)

        tail_at = full * n * per - (n // 2 * per if s >= n // 2 else 0)
        return jnp.concatenate([gather(f * n * per) for f in range(full)] + [gather(tail_at)], axis=1)

    def coefficients(rb):
        wide = dot_nt(rb, basis[...])
        lane = lanes_of(wide)
        low = jnp.where(lane < nc, wide, 0.0).astype(BF16)
        high = jnp.where((lane < full * LANES) | (lane >= nc), wide, 0.0).astype(BF16)
        return low, high

    def main_parts(it, sides):
        for s in range(n):
            wide = dot_nt(sides[s >= n // 2], stack(s, 0, full * LANES))
            wide = jnp.concatenate([wide[:, f * LANES : (f + 1) * LANES] for f in range(full)], axis=0)
            part_out[it, s + 1, pl.ds(0, mains)] = wide.astype(BF16)

    def tail_parts(it, sides):
        for s in range(n):
            block = stack(s, nc - TAIL, nc)
            tail = dot_nt(sides[s >= n // 2], jnp.concatenate([block, block], axis=0))
            part_out[it, s + 1, pl.ds(mains, rows // 2)] = fold_tail(tail).astype(BF16)

    def whole_parts(it, sides):
        for s in range(n):
            block = stack(s, 0, nc)
            wide = dot_nt(sides[s >= n // 2], jnp.concatenate([block, block[nc - TAIL :]], axis=0))
            part_out[it, s + 1] = fold(wide, full).astype(BF16)
            for peer in (s - 1, s) if s % 2 == 0 else (s,) if s == n - 1 else ():
                if peer >= 0:
                    @pl.when(me_s != peer)
                    def _():
                        part_copy(it, peer, me_s, 2).start()

    def gathered(it, lines):
        total = part_in[it, 0, :, lines].astype(F32)
        for s in range(1, n):
            total = total + part_in[it, s, :, lines].astype(F32)
        return total

    def coarse(it, count):
        total = part_in[it, 0, 0:count].astype(F32)
        for s in range(1, n):
            total = total + part_in[it, s, 0:count].astype(F32)
        return [unfold(total[i], rows, full).astype(BF16) for i in range(count)]

    def lift_operator():
        row = lax.broadcasted_iota(jnp.int32, (deep, nc), 0)
        row = jnp.where(row < nc, row, row - TAIL)
        source = row
        for i in range(m):
            here = (row >= i * per) & (row < (i + 1) * per)
            source = jnp.where(here, row + (order[i] - i) * per, source)
        place = (lax.broadcasted_iota(jnp.int32, (deep, nc), 1) == source).astype(F32).astype(BF16)

        def put(i, value):
            value = dot(place, value.astype(BF16)).astype(BF16)
            lifted[pl.ds(pl.multiple_of(i * deep, deep), deep), :] = value

        raised[...] = dot(place, basis[:nc]).astype(BF16)
        put(1, dot(basis[:nc], diag[...]))
        for side, i in ((NEAR, 2 * (1 - odd)), (FAR, 2 * odd)):
            arrive(near_copy, 0, side)
            put(i, dot(near[side], rim[part[side], :]))

    def permuted_inverse():
        used = ov[...]
        slot = lax.broadcasted_iota(jnp.int32, used.shape, 1)
        used = jnp.where(slot < count[...], used, -1)
        chunk = 2 * h // 4
        for i in range(4):
            place = lax.broadcasted_iota(jnp.int32, (chunk, slots), 0) + i * chunk
            pick = (place == used).astype(F32).astype(BF16)
            invp[i * chunk : (i + 1) * chunk, :] = dot(pick, inv[half:, :]).astype(BF16)
            if i > 0:
                relay(i - 1, i)

    def own_and_near(e, weights, margin):
        base[...] = dot(sent[e], weights)
        arrive(halo_copy, e, NEAR)
        base[...] += dot(halo[e, NEAR], margin[part[NEAR], :])

    def far_part(e, margin, columns):
        return dot(halo[e, FAR], margin[part[FAR], columns])

    def residual(e, columns, product):
        v = cur[:, columns]
        sent[e, :, columns] = (load[:, columns] - product - cubic_coef * v * v * v).astype(BF16)

    get_diag.wait()
    base[...] = dot(sent[0], diag[...])
    up_maps(lambda copy: copy.start(), True)
    get_basis.wait()
    get_again.wait()
    begin(near_copy, 0, FAR)
    begin(near_copy, 0, NEAR)
    get_rim.wait()
    arrive(halo_copy, 0, NEAR)
    base[...] += dot(halo[0, NEAR], rim[part[NEAR], :])
    get_load.wait()
    arrive(halo_copy, 0, FAR)
    for side in (FAR, NEAR):
        residual(1, part[side], base[:, part[side]] + far_part(0, rim, part[side]))
        begin(halo_copy, 1, side)

    for it in range(ITERS):
        first, last = it == 0, it == ITERS - 1
        e = 2 * it + 1
        if first:
            get_inv.wait()
            get_ov.wait()
            get_count.wait()
            permuted_inverse()
        else:
            whole_parts(it, coefficients(sent[e]))
            part_in[it, me_s, 0:2] = part_out[it, pl.ds(me_s + odd, 2)]
        own_and_near(e, inv[:half, :], invp)
        if first:
            relay(3, pieces)
        arrive(halo_copy, e, FAR)
        for side in (FAR, NEAR):
            v = cur[:, part[side]] + (base[:, part[side]] + far_part(e, invp, part[side]))
            cur[:, part[side]] = v
            sent[e + 1, :, part[side]] = v.astype(BF16)
            if first or side == FAR:
                begin(halo_copy, e + 1, side)
        if first:
            sides = coefficients(sent[e])
            maps_wait(0, early)
            main_parts(it, sides)
            part_start(it, 0)
            maps_wait(early, m)
            tail_parts(it, sides)
            part_start(it, 1)
            part_in[it, me_s] = part_out[it, pl.ds(me_s, 3)]
            own_and_near(e + 1, diag[...], rim)
            lift_operator()
            e = e + 1
            arrive(halo_copy, e, FAR)
            base[...] += far_part(e, rim, slice(None))
            part_wait(it, 0)
            total = [gathered(it, pl.ds(0, mains))]
            part_wait(it, 1)
            total = jnp.concatenate(total + [gathered(it, pl.ds(mains, rows // 2))], axis=1)
            three = [unfold(total[i], rows, full).astype(BF16) for i in range(3)]
            mine, three = three[1], jnp.concatenate(three, axis=1)
            for side in (FAR, NEAR):
                cur[:, part[side]] += dot(mine, raised[:, part[side]])
                residual(e + 1, part[side], base[:, part[side]] + dot(three, lifted[:, part[side]]))
                begin(halo_copy, e + 1, side)
        else:
            e = e + 1
            base[...] = dot(sent[e], diag[...])
            part_wait(it, 2)
            pair = coarse(it, 2)
            mine = jnp.where(odd == 1, pair[0].astype(F32), pair[1].astype(F32)).astype(BF16)
            for side in (NEAR, FAR):
                columns = part[side]
                change = dot(mine, raised[:, columns])
                v = cur[:, columns]
                if last:
                    before_ref[:, columns] = v
                    change_ref[:, columns] = change
                else:
                    cur[:, columns] = v + change
                if side == NEAR:
                    sent[e, :, columns] = (v + change).astype(BF16)
                    begin(halo_copy, e, NEAR)
            both = pl.ds(pl.multiple_of(odd * deep, deep), 2 * deep)
            base[...] += dot(jnp.concatenate(pair, axis=1), lifted[both, :])
            arrive(halo_copy, e, NEAR)
            base[...] += dot(halo[e, NEAR], rim[part[NEAR], :])
            arrive(halo_copy, e, FAR)
            for side in (FAR, NEAR):
                product = base[:, part[side]] + far_part(e, rim, part[side])
                if last:
                    applied_ref[:, part[side]] = product
                else:
                    residual(e + 1, part[side], product)
                    begin(halo_copy, e + 1, side)

    for side in (FAR, NEAR):
        for e in range(2 * ITERS + 1):
            finish(halo_copy, e, side)
        finish(near_copy, 0, side)
    down_maps(lambda copy: copy.wait_send())
    up_maps(lambda copy: copy.wait_send(), False)
    relay_done()
    for it in range(ITERS):
        for kind in (0, 1) if it == 0 else (2,):
            for k in range(1, n):
                part_copy(it, lax.rem(me_s + k, n), me_s, kind).wait_send()


def body(n, m, state_init, load_cols, stiff_diag, stiff_rim, inverse, ov_rows, ov_count, coarse_basis, coarse_map):
    rows, width = state_init.shape
    h = stiff_rim.shape[0] // 2
    basis_t = coarse_basis.T
    nc = basis_t.shape[0]
    if nc % LANES != TAIL or n % 2 or rows % 32 or width != 2 * h:
        raise ValueError("unsupported sizes")
    full = nc // LANES
    trades = 2 * ITERS + 1
    packed = (rows * full + rows // 2, LANES)
    hbm = pl.BlockSpec(memory_space=pltpu.HBM)
    vmem = pl.BlockSpec(memory_space=pltpu.VMEM)
    dma = pltpu.SemaphoreType.DMA
    out = jax.ShapeDtypeStruct((rows, width), F32)
    before, change, product = pl.pallas_call(
        functools.partial(kernel, n, m),
        out_shape=(out, out, out),
        in_specs=[hbm] * 9,
        out_specs=(vmem, vmem, vmem),
        scratch_shapes=[
            pltpu.VMEM((rows, width), F32),
            pltpu.VMEM((rows, width), F32),
            pltpu.VMEM((rows, width), F32),
            pltpu.VMEM(stiff_diag.shape, BF16),
            pltpu.VMEM(stiff_rim.shape, BF16),
            pltpu.VMEM(inverse.shape, BF16),
            pltpu.VMEM(ov_rows.shape, jnp.int32),
            pltpu.VMEM((1, 1), jnp.int32),
            pltpu.VMEM((nc + TAIL, width), BF16),
            pltpu.VMEM((nc + TAIL, width), BF16),
            pltpu.VMEM((2, nc, h), BF16),
            pltpu.VMEM((3 * (nc + TAIL), width), BF16),
            pltpu.VMEM(coarse_map.shape, BF16),
            pltpu.VMEM((m, coarse_map.shape[1] * full + coarse_map.shape[1] // 2, LANES), BF16),
            pltpu.VMEM((2 * h, width), BF16),
            pltpu.VMEM((trades, rows, width), BF16),
            pltpu.VMEM((trades, 2, rows, h), BF16),
            pltpu.VMEM((ITERS, n + 2) + packed, BF16),
            pltpu.VMEM((ITERS, n, 3) + packed, BF16),
            dma((10,)),
            dma((trades, 2)),
            dma((trades, 2)),
            dma((2,)),
            dma((2,)),
            dma((m, PIECES)),
            dma((m, PIECES)),
            dma((PIECES,)),
            dma((ITERS, 2, n)),
            dma((ITERS, 2, n)),
            pltpu.SemaphoreType.REGULAR((m,)),
        ],
        compiler_params=pltpu.CompilerParams(collective_id=0, has_side_effects=True, vmem_limit_bytes=60 * 2**20),
        name="schwarz",
    )(state_init, load_cols, stiff_diag, stiff_rim, inverse, ov_rows, ov_count.reshape(1, 1), basis_t, coarse_map)
    current = before + change
    return current, load_cols - product - cubic_coef * current * current * current


def solution(mesh):
    in_specs = (
        P("col", "sub"),
        P("col", "sub"),
        P(None, "sub"),
        P(None, "sub"),
        P(None, "sub"),
        P("sub", None),
        P("sub"),
        P("sub", None),
        P("sub", "col"),
    )
    out_specs = (P("col", "sub"), P("col", "sub"))
    step = functools.partial(body, mesh.shape["sub"], mesh.shape["col"])
    return jax.shard_map(step, mesh=mesh, in_specs=in_specs, out_specs=out_specs, check_vma=False)
```
